256 devices in a mesh: dp: 16 (over x, y), table: 16 (over z, core).
Axes of the slice: x: 4, y: 4, z: 8, core: 2. Of those that a mesh axis runs over, the one named last changes fastest.
Arguments:
- item_ids: int32 [65536], P('dp'), may hold values from 0 to 32767
- user_len: int32 [256], P('dp'), may hold values from 32 to 256
- emb_table: bfloat16 [512, 32768], P('table'), may hold values from -6 to 6
- cotangent: bfloat16 [512, 65536], P('table', 'dp'), may hold values from -6 to 6
- w_uvqk: bfloat16 [512, 2048], replicated, may hold values from -0.25 to 0.25
- w_out: bfloat16 [512, 512], replicated, may hold values from -0.25 to 0.25
- gain_in: float32 [512], replicated, may hold values from 0.25 to 1.75
- gain_mid: float32 [512], replicated, may hold values from 0.25 to 1.75
Outputs:
- layer_out: bfloat16 [512, 65536], P('table', 'dp')
- table_grad: float32 [512, 32768], P('table', 'dp')
The draws below stay inside these ranges and needn't reach their ends.
All inputs are finite; a program needn't handle non-finite values.
Results may differ from the reference program's by a relative error of at most 0.012.
Values may be sent and summed in bfloat16 or wider, within the bound.
A program may use at most 128 MiB of HBM per device.

```python
import math
import jax
import jax.numpy as jnp
import numpy as np
from jax import lax

D = 512
HEADS = 8
SLOT = 256
VOCAB = 32768
SLOTS_DEV = 1
USERS = 256
ROWS = 65536


def plant(drawn, rng, least, top_value):
    spot = [jax.random.randint(jax.random.fold_in(rng, axis), (), 0, length) for axis, length in enumerate(drawn.shape)]
    widest = drawn.shape.index(max(drawn.shape))
    neighbour = spot[:widest] + [(spot[widest] + 1) % drawn.shape[widest]] + spot[widest + 1:]
    return drawn.at[tuple(spot)].set(least).at[tuple(neighbour)].set(top_value)


def level_of(own_key, shape, cuts, least, largest):
    level = 1.0
    for position, shards_of in cuts:
        heights = jax.random.uniform(jax.random.fold_in(jax.random.fold_in(own_key, 6), position), (shards_of,), jnp.float32, least / len(cuts), largest / len(cuts))
        level = level * jnp.repeat(jnp.exp(heights), shape[position] // shards_of).reshape((-1,) + (1,) * (len(shape) - 1 - position))
    return level


def cumulative_ranks(number_of, skew):
    loads = [(1 << 20) // math.isqrt(standing ** skew) + 1 for standing in range(1, number_of + 1)]
    scale = 1 + sum(loads) // (1 << 30)
    return np.cumsum(np.array([max(1, weight // scale) for weight in loads]))


def skewed_ids(rng, dims, amount, slope):
    grid = cumulative_ranks(amount, slope)
    pick = jax.random.randint(jax.random.fold_in(rng, 1), dims, 0, int(grid[amount - 1]))
    rank = jnp.searchsorted(jnp.asarray(grid, jnp.int32), pick, side="right")
    return jax.random.permutation(jax.random.fold_in(rng, 2), amount)[rank].astype(jnp.int32)


def gaussian(own_key, dims, scale, most, split=(), kind=jnp.bfloat16):
    result = scale * jax.random.normal(own_key, dims, jnp.float32)
    if split:
        result = result * level_of(own_key, dims, split, -0.22, 0.18)
    return jnp.clip(result, -most, most).astype(kind)


def setup_inputs(seed: int = 0) -> dict:
    key_list = jax.random.split(jax.random.key(seed), 9)
    item_ids = plant(skewed_ids(key_list[0], (ROWS,), VOCAB, 2), jax.random.fold_in(key_list[0], 3), 0, VOCAB - 1).astype(jnp.int32)
    user_len = plant(jax.random.randint(key_list[1], (USERS,), SLOT // 8, SLOT + 1), jax.random.fold_in(key_list[1], 1), SLOT // 8, SLOT).astype(jnp.int32)
    emb_table = gaussian(key_list[2], (D, VOCAB), 1.0, 6.0, ((0, 16),))
    cotangent = gaussian(key_list[3], (D, ROWS), 1.0, 6.0, ((0, 16), (1, 16)))
    w_uvqk = gaussian(key_list[4], (D, 4 * D), D ** -0.5, 0.25)
    w_out = gaussian(key_list[5], (D, D), D ** -0.5, 0.25)
    gain_in = jnp.clip(1.0 + 0.15 * jax.random.normal(key_list[6], (D,), jnp.float32), 0.25, 1.75)
    gain_mid = jnp.clip(1.0 + 0.15 * jax.random.normal(key_list[7], (D,), jnp.float32), 0.25, 1.75)
    return {"item_ids": item_ids, "user_len": user_len, "emb_table": emb_table, "cotangent": cotangent, "w_uvqk": w_uvqk, "w_out": w_out, "gain_in": gain_in, "gain_mid": gain_mid}


norm_eps = 1e-05

def row_norm(values, gain):
    centred = values - lax.optimization_barrier(jnp.mean(values, axis=-1, keepdims=True))
    spread_sq = lax.optimization_barrier(jnp.mean(centred * centred, axis=-1, keepdims=True))
    return centred * lax.rsqrt(spread_sq + norm_eps) * gain

def hstu_layer(embedded, lengths, w_uvqk, w_out, gain_in, gain_mid):
    slots, positions, width = embedded.shape
    head_dim = width // HEADS
    widened = embedded.astype(jnp.float32)
    normed = row_norm(widened, gain_in).astype(jnp.bfloat16)
    projected = jnp.dot(normed.reshape(-1, width), w_uvqk, preferred_element_type=jnp.float32)
    projected = jax.nn.silu(projected).astype(jnp.bfloat16).reshape(slots, positions, 4, HEADS, head_dim)
    gate_rows = projected[:, :, 0].reshape(slots, positions, width)
    value_rows = projected[:, :, 1].astype(jnp.float32)
    queries = projected[:, :, 2].astype(jnp.float32)
    key_rows = projected[:, :, 3].astype(jnp.float32)
    scores = jnp.einsum('sqhd,skhd->shqk', queries, key_rows) * head_dim ** (-0.5)
    order = jnp.arange(positions, dtype=jnp.int32)
    causal = order[None, :] <= order[:, None]
    key_mask = causal[None, :, :] & (order[None, None, :] < lengths[:, None, None])
    divisor = lengths.astype(jnp.float32)[:, None, None, None]
    weights = jnp.where(key_mask[:, None], jax.nn.silu(scores), 0.0) / divisor
    weights = weights.astype(jnp.bfloat16).astype(jnp.float32)
    attended = jnp.einsum('shqk,skhd->sqhd', weights, value_rows).reshape(slots, positions, width)
    mixed = (row_norm(attended, gain_mid) * gate_rows.astype(jnp.float32)).astype(jnp.bfloat16)
    update = jnp.dot(mixed.reshape(-1, width), w_out, preferred_element_type=jnp.float32)
    return (widened + update.reshape(slots, positions, width)).astype(jnp.bfloat16)

def reference(item_ids, user_len, emb_table, cotangent, w_uvqk, w_out, gain_in, gain_mid):
    user_count = user_len.shape[0]
    groups = user_count // SLOTS_DEV
    embedded = emb_table.T[item_ids].reshape(groups, SLOTS_DEV, SLOT, D)
    cot_rows = cotangent.T.reshape(groups, SLOTS_DEV, SLOT, D)
    lengths = user_len.reshape(groups, SLOTS_DEV)

    def one_group(packed):
        rows_in, cot_in, lens_in = packed
        order = jnp.arange(SLOT, dtype=jnp.int32)
        valid_rows = order[None, :] < lens_in[:, None]
        masked = jnp.where(valid_rows[:, :, None], cot_in, jnp.zeros_like(cot_in))

        def forward(values):
            return hstu_layer(values, lens_in, w_uvqk, w_out, gain_in, gain_mid)
        layer_rows, pullback = jax.vjp(forward, rows_in)
        return (layer_rows, pullback(masked)[0])
    layer_rows, row_grad = lax.map(one_group, (embedded, cot_rows, lengths))
    layer_out = layer_rows.reshape(-1, D).T
    table_grad = jax.ops.segment_sum(row_grad.reshape(-1, D).astype(jnp.float32), item_ids, num_segments=VOCAB)
    return (layer_out, table_grad.T)
```

```python
import functools

import jax
import jax.numpy as jnp
from jax import lax
from jax.experimental import pallas as pl
from jax.experimental.pallas import tpu as pltpu
from jax.sharding import PartitionSpec as P

F32, BF16, I32 = jnp.float32, jnp.bfloat16, jnp.int32
MESH = pl.DeviceIdType.MESH
VM = pl.BlockSpec(memory_space=pltpu.VMEM)
SM = pl.BlockSpec(memory_space=pltpu.SMEM)
EPS = 1e-5
HEADS = 8
NN = (((1,), (0,)), ((), ()))
TN = (((0,), (0,)), ((), ()))
NT = (((1,), (1,)), ((), ()))
TABLE = 16
SIDE = 4


def mm(a, b, dims):
    return lax.dot_general(a, b, dims, preferred_element_type=F32)


def sigmoid(z):
    return 0.5 * jnp.tanh(0.5 * z) + 0.5


def place():
    d, t = lax.axis_index("dp"), lax.axis_index("table")
    return d, t, d // SIDE, d % SIDE


def table_peer(t, j):
    return (t + TABLE + TABLE // 2 + (1 - 2 * (j % 2)) * ((j + 1) // 2)) % TABLE


def greet(d, t, xq, yq, with_sides):
    bar = pltpu.get_barrier_semaphore()

    def signal(j, c):
        pl.semaphore_signal(bar, inc=1, device_id=(d, table_peer(t, j)), device_id_type=MESH)
        return c

    lax.fori_loop(0, TABLE - 1, signal, 0)
    if with_sides:
        for q in range(1, SIDE):
            for peer in (xq * SIDE + (yq + q) % SIDE, ((xq + q) % SIDE) * SIDE + yq):
                pl.semaphore_signal(bar, inc=1, device_id=(peer, t), device_id_type=MESH)
    return bar, TABLE - 1 + (2 * (SIDE - 1) if with_sides else 0)


HI = 16


def gather_block(ids, table_ref):
    oh = jnp.where(lax.broadcasted_iota(I32, (256, 256), 0) == (ids & 255), 1.0, 0.0).astype(BF16)
    hi = jnp.broadcast_to(ids >> 8, (32, 256))
    acc = jnp.zeros((32, 256), F32)
    for m in range(table_ref.shape[1] // (256 * HI)):
        lhs = jnp.concatenate(
            [table_ref[:, (m * HI + q) * 256 : (m * HI + q + 1) * 256] for q in range(HI)], axis=0
        )
        part = mm(lhs, oh, NN)
        for q in range(HI):
            acc = jnp.where(hi == m * HI + q, part[q * 32 : (q + 1) * 32], acc)
    return acc.astype(BF16)


def enter_kernel(ids_ref, table_ref, cot_ref, x_ref, c_ref, ida_ref, idb_ref, stage,
                 esend, erecv, csend, crecv, isend, irecv):
    d, t, xq, yq = place()
    bar, count = greet(d, t, xq, yq, True)

    def block(j):
        u = table_peer(t, j)
        return gather_block(ids_ref[:, pl.ds(pl.multiple_of(u * 256, 256), 256)], table_ref)

    mine = pl.ds(pl.multiple_of(t * 32, 32), 32)

    def emb_copy(j):
        return pltpu.make_async_remote_copy(
            src_ref=stage.at[j], dst_ref=x_ref.at[mine, :], send_sem=esend.at[j], recv_sem=erecv.at[j],
            device_id=(d, table_peer(t, j)), device_id_type=MESH)

    def cot_copy(j):
        u = table_peer(t, j)
        return pltpu.make_async_remote_copy(
            src_ref=cot_ref.at[:, pl.ds(pl.multiple_of(u * 256, 256), 256)], dst_ref=c_ref.at[mine, :],
            send_sem=csend.at[j], recv_sem=crecv.at[j], device_id=(d, u), device_id_type=MESH)

    def id_copies():
        out = []
        for q in range(1, SIDE):
            out.append(pltpu.make_async_remote_copy(
                src_ref=ids_ref, dst_ref=ida_ref.at[yq], send_sem=isend.at[0, q], recv_sem=irecv.at[0, q],
                device_id=(xq * SIDE + (yq + q) % SIDE, t), device_id_type=MESH))
            out.append(pltpu.make_async_remote_copy(
                src_ref=ids_ref, dst_ref=idb_ref.at[xq], send_sem=isend.at[1, q], recv_sem=irecv.at[1, q],
                device_id=(((xq + q) % SIDE) * SIDE + yq, t), device_id_type=MESH))
        return out

    stage[0] = block(0)
    pl.semaphore_wait(bar, count)
    emb_copy(0).start()
    cot_copy(0).start()
    for c in id_copies():
        c.start()

    def step(j, c):
        stage[j] = block(j)

        @pl.when(j < TABLE - 1)
        def _():
            emb_copy(j).start()
            cot_copy(j).start()

        return c

    lax.fori_loop(1, TABLE, step, 0)
    x_ref[mine, :] = stage[TABLE - 1]
    c_ref[mine, :] = cot_ref[:, pl.ds(pl.multiple_of(t * 256, 256), 256)]
    ida_ref[yq] = ids_ref[...]
    idb_ref[xq] = ids_ref[...]

    def finish(j, c):
        emb_copy(j).wait()
        cot_copy(j).wait()
        return c

    lax.fori_loop(0, TABLE - 1, finish, 0)
    for c in id_copies():
        c.wait()


def enter(ids, table, cot):
    f, n = cot.shape
    sem = pltpu.SemaphoreType.DMA
    return pl.pallas_call(
        enter_kernel,
        out_shape=(jax.ShapeDtypeStruct((TABLE * f, 256), BF16), jax.ShapeDtypeStruct((TABLE * f, 256), BF16),
                   jax.ShapeDtypeStruct((SIDE, 1, n), I32), jax.ShapeDtypeStruct((SIDE, 1, n), I32)),
        in_specs=[VM] * 3,
        out_specs=(VM,) * 4,
        scratch_shapes=[pltpu.VMEM((TABLE, f, 256), BF16)] + [sem((TABLE,))] * 4 + [sem((2, SIDE))] * 2,
        compiler_params=pltpu.CompilerParams(collective_id=0, has_side_effects=True, vmem_limit_bytes=60 << 20),
    )(ids.reshape(1, n), table, cot)


def column(row):
    n = row.shape[1]
    tall = jnp.broadcast_to(row, (128, n)).T
    return jnp.concatenate([tall, tall], axis=1)

def layer_kernel(len_ref, x_ref, c_ref, w_ref, wo_ref, gin_ref, gmid_ref, out_ref, grad_ref,
                 p_ref, zd_ref, dz_ref, wt_ref, sd_ref, a_ref):
    D, S = x_ref.shape
    hd = D // HEADS
    ln = len_ref[lax.axis_index("table")]
    x = x_ref[...].astype(F32)
    mu = jnp.mean(x, axis=0, keepdims=True)
    cen = x - mu
    r1 = lax.rsqrt(jnp.mean(cen * cen, axis=0, keepdims=True) + EPS)
    gin = column(gin_ref[...])
    gmid = column(gmid_ref[...])
    normed = (cen * r1 * gin).astype(BF16)
    for b in range(4):
        z = mm(w_ref[:, b * D:(b + 1) * D], normed, TN)
        sg = sigmoid(z)
        p_ref[b * D:(b + 1) * D, :] = (z * sg).astype(BF16)
        zd_ref[b * D:(b + 1) * D, :] = sg * (1.0 + z * (1.0 - sg))
    key_i = lax.broadcasted_iota(jnp.int32, (S, S), 0)
    qry_i = lax.broadcasted_iota(jnp.int32, (S, S), 1)
    inv = 1.0 / jnp.full((S, S), ln, jnp.int32).astype(F32)
    scale = jnp.where((key_i <= qry_i) & (key_i < ln), inv, 0.0)
    for h in range(HEADS):
        vT = p_ref[D + h * hd:D + (h + 1) * hd, :]
        qT = p_ref[2 * D + h * hd:2 * D + (h + 1) * hd, :]
        kT = p_ref[3 * D + h * hd:3 * D + (h + 1) * hd, :]
        s = mm(kT, qT, TN) * (hd ** -0.5)
        sg = sigmoid(s)
        wt = (s * sg * scale).astype(BF16)
        wt_ref[h] = wt
        sd_ref[h] = sg * (1.0 + s * (1.0 - sg)) * (scale * hd ** -0.5)
        a_ref[h * hd:(h + 1) * hd, :] = mm(vT, wt, NN)
    a = a_ref[...]
    cen2 = a - jnp.mean(a, axis=0, keepdims=True)
    r2 = lax.rsqrt(jnp.mean(cen2 * cen2, axis=0, keepdims=True) + EPS)
    nh2 = cen2 * r2
    u = p_ref[0:D, :].astype(F32)
    mixed = (nh2 * gmid * u).astype(BF16)
    out_ref[...] = (x_ref[...].astype(F32) + mm(wo_ref[...], mixed, TN)).astype(BF16)
    pos = lax.broadcasted_iota(jnp.int32, (D, S), 1)
    g32 = jnp.where(pos < ln, c_ref[...].astype(F32), 0.0)
    g = g32.astype(BF16)
    dm = mm(wo_ref[...], g, NN).astype(BF16).astype(F32)
    dz_ref[0:D, :] = ((dm * nh2 * gmid).astype(BF16).astype(F32) * zd_ref[0:D, :]).astype(BF16)
    dn = dm * u * gmid
    da = r2 * (dn - jnp.mean(dn, axis=0, keepdims=True) - nh2 * jnp.mean(dn * nh2, axis=0, keepdims=True))
    a_ref[...] = da
    for h in range(HEADS):
        vT = p_ref[D + h * hd:D + (h + 1) * hd, :]
        qT = p_ref[2 * D + h * hd:2 * D + (h + 1) * hd, :]
        kT = p_ref[3 * D + h * hd:3 * D + (h + 1) * hd, :]
        dah = a_ref[h * hd:(h + 1) * hd, :].astype(BF16)
        wt = wt_ref[h]
        dw = mm(vT, dah, TN).astype(BF16).astype(F32)
        ds = (dw * sd_ref[h]).astype(BF16)
        for b, val in ((1, mm(dah, wt, NT)), (2, mm(kT, ds, NN)), (3, mm(qT, ds, NT))):
            rows = slice(b * D + h * hd, b * D + (h + 1) * hd)
            dz_ref[rows, :] = (val.astype(BF16).astype(F32) * zd_ref[rows, :]).astype(BF16)
    dnr = mm(w_ref[...], dz_ref[...], NN).astype(BF16).astype(F32) * gin
    x = x_ref[...].astype(F32)
    nh1 = (x - mu) * r1
    de = r1 * (dnr - jnp.mean(dnr, axis=0, keepdims=True) - nh1 * jnp.mean(dnr * nh1, axis=0, keepdims=True))
    grad_ref[...] = (de + g32).astype(BF16)


def layer(user_len, xT, cT, w, wo, gin, gmid):
    D, S = xT.shape
    return pl.pallas_call(
        layer_kernel,
        out_shape=(jax.ShapeDtypeStruct((D, S), BF16),) * 2,
        in_specs=[SM] + [VM] * 6,
        out_specs=(VM, VM),
        scratch_shapes=[pltpu.VMEM((4 * D, S), BF16), pltpu.VMEM((4 * D, S), F32), pltpu.VMEM((4 * D, S), BF16),
                        pltpu.VMEM((HEADS, S, S), BF16), pltpu.VMEM((HEADS, S, S), F32), pltpu.VMEM((D, S), F32)],
        compiler_params=pltpu.CompilerParams(vmem_limit_bytes=60 << 20),
    )(user_len, xT, cT, w, wo, gin.reshape(1, D), gmid.reshape(1, D))


CHUNK = 2048


def scatter_block(hi, lo, g):
    k = g.shape[1]
    oht = jnp.where(lax.broadcasted_iota(I32, (256, k), 0) == lo, 1.0, 0.0).astype(BF16)
    hib = jnp.broadcast_to(hi.astype(F32).astype(BF16), (16, k))
    zero = jnp.zeros((16, k), BF16)
    lhs = jnp.concatenate([jnp.where(hib == jnp.array(q, BF16), g, zero) for q in range(32)], axis=0)
    return mm(lhs, oht, NT)


def leave_kernel(o_ref, g_ref, ida_ref, idb_ref, out_ref, sum_ref, home, ga, gb, acca, accb, sa, sb, ra, rb,
                 osend, orecv, gsend, grecv, asend, arecv, rsend, rrecv):
    d, t, xq, yq = place()
    bar, count = greet(d, t, xq, yq, True)
    here = pl.ds(pl.multiple_of(t * 256, 256), 256)

    def copy(j, src, dst, send, recv):
        u = table_peer(t, j)
        return pltpu.make_async_remote_copy(
            src_ref=src.at[pl.ds(pl.multiple_of(u * 32, 32), 32), :], dst_ref=dst.at[:, here],
            send_sem=send.at[j], recv_sem=recv.at[j], device_id=(d, u), device_id_type=MESH)

    def gcopy(j):
        return copy(j, g_ref, home, gsend, grecv)

    def ocopy(j):
        return copy(j, o_ref, out_ref, osend, orecv)

    pl.semaphore_wait(bar, count)
    lax.fori_loop(0, TABLE - 1, lambda j, c: (gcopy(j).start(), c)[1], 0)
    lax.fori_loop(0, TABLE - 1, lambda j, c: (ocopy(j).start(), c)[1], 0)
    mine = pl.ds(pl.multiple_of(t * 32, 32), 32)
    home[:, here] = g_ref[mine, :]
    out_ref[:, here] = o_ref[mine, :]
    acca[...] = jnp.zeros_like(acca)
    accb[...] = jnp.zeros_like(accb)
    lax.fori_loop(0, TABLE - 1, lambda j, c: (gcopy(j).wait(), c)[1], 0)

    def peers(q):
        return xq * SIDE + (yq + q) % SIDE, ((xq + q) % SIDE) * SIDE + yq

    def rows(q):
        pa, pb = peers(q)
        return (
            pltpu.make_async_remote_copy(
                src_ref=home.at[0:16, :], dst_ref=ga.at[q], send_sem=asend.at[0, q], recv_sem=arecv.at[0, q],
                device_id=(pa, t), device_id_type=MESH),
            pltpu.make_async_remote_copy(
                src_ref=home.at[16:32, :], dst_ref=gb.at[q], send_sem=asend.at[1, q], recv_sem=arecv.at[1, q],
                device_id=(pb, t), device_id_type=MESH))

    for q in range(1, SIDE):
        for c in rows(q):
            c.start()

    n = home.shape[1]

    def add_a(ids, g):
        hi = jnp.where(((ids >> 11) & 3) == yq, (ids >> 13) * 8 + ((ids >> 8) & 7), -1)
        acca[...] += scatter_block(hi, ids & 255, g)

    def add_b(ids, g):
        hi = jnp.where((ids >> 13) == xq, (ids >> 8) & 31, -1)
        accb[...] += scatter_block(hi, ids & 255, g)

    def over(fn):
        def body(i, c):
            fn(pl.ds(pl.multiple_of(i * CHUNK, CHUNK), CHUNK))
            return c

        lax.fori_loop(0, n // CHUNK, body, 0)

    def both(at):
        add_a(ida_ref[yq, :, at], home[0:16, at])
        add_b(idb_ref[xq, :, at], home[16:32, at])

    over(both)

    def sums(half, q, acc, send, recv):
        to = (xq + q) % SIDE if half == 0 else (yq + q) % SIDE
        peer = peers(q)[1 - half]
        return pltpu.make_async_remote_copy(
            src_ref=send.at[pl.ds(pl.multiple_of(to * 128, 128), 128), :], dst_ref=recv.at[q],
            send_sem=rsend.at[half, q], recv_sem=rrecv.at[half, q], device_id=(peer, t), device_id_type=MESH)

    for q in range(1, SIDE):
        rows(q)[0].wait()
        over(lambda at: add_a(ida_ref[(yq + SIDE - q) % SIDE, :, at], ga[q, :, at]))
    sa[...] = acca[...].astype(BF16)
    for q in range(1, SIDE):
        sums(0, q, acca, sa, ra).start()
    for q in range(1, SIDE):
        rows(q)[1].wait()
        over(lambda at: add_b(idb_ref[(xq + SIDE - q) % SIDE, :, at], gb[q, :, at]))
    sb[...] = accb[...].astype(BF16)
    for q in range(1, SIDE):
        sums(1, q, accb, sb, rb).start()
    for half, acc, recv, send, own in ((0, acca, ra, sa, xq), (1, accb, rb, sb, yq)):
        total = acc[pl.ds(pl.multiple_of(own * 128, 128), 128), :]
        for q in range(1, SIDE):
            sums(half, q, acc, send, recv).wait()
            total = total + recv[q].astype(F32)
        for h in range(8):
            sum_ref[half * 16 : half * 16 + 16, h * 256 : (h + 1) * 256] = total[h * 16 : (h + 1) * 16]
    lax.fori_loop(0, TABLE - 1, lambda j, c: (ocopy(j).wait(), c)[1], 0)


def leave(oT, gT, ida, idb, vocab):
    n = ida.shape[2]
    sem = pltpu.SemaphoreType.DMA
    return pl.pallas_call(
        leave_kernel,
        out_shape=(jax.ShapeDtypeStruct((32, n), BF16), jax.ShapeDtypeStruct((32, vocab), F32)),
        in_specs=[VM] * 4,
        out_specs=(VM, VM),
        scratch_shapes=[pltpu.VMEM((32, n), BF16), pltpu.VMEM((SIDE, 16, n), BF16), pltpu.VMEM((SIDE, 16, n), BF16),
                        pltpu.VMEM((512, 256), F32), pltpu.VMEM((512, 256), F32),
                        pltpu.VMEM((512, 256), BF16), pltpu.VMEM((512, 256), BF16),
                        pltpu.VMEM((SIDE, 128, 256), BF16), pltpu.VMEM((SIDE, 128, 256), BF16)]
        + [sem((TABLE,))] * 4 + [sem((2, SIDE))] * 4,
        compiler_params=pltpu.CompilerParams(collective_id=1, has_side_effects=True, vmem_limit_bytes=60 << 20),
    )(oT, gT, ida, idb)


def on_device(item_ids, user_len, emb_table, cotangent, w_uvqk, w_out, gain_in, gain_mid):
    xT, cT, ida, idb = enter(item_ids, emb_table, cotangent)
    oT, gT = layer(user_len, xT, cT, w_uvqk, w_out, gain_in, gain_mid)
    return leave(oT, gT, ida, idb, emb_table.shape[1] // lax.axis_size("dp"))


def solution(mesh):
    return jax.shard_map(
        on_device,
        mesh=mesh,
        in_specs=(P("dp"), P("dp"), P("table", None), P("table", "dp"), P(), P(), P(), P()),
        out_specs=(P("table", "dp"), P("table", "dp")),
        check_vma=False,
    )
```

```python
import functools

import jax
import jax.numpy as jnp
from jax import lax
from jax.experimental import pallas as pl
from jax.experimental.pallas import tpu as pltpu
from jax.sharding import PartitionSpec as P

F32, BF16, I32 = jnp.float32, jnp.bfloat16, jnp.int32
MESH = pl.DeviceIdType.MESH
VM = pl.BlockSpec(memory_space=pltpu.VMEM)
SM = pl.BlockSpec(memory_space=pltpu.SMEM)
EPS = 1e-5
HEADS = 8
NN = (((1,), (0,)), ((), ()))
TN = (((0,), (0,)), ((), ()))
NT = (((1,), (1,)), ((), ()))
TABLE = 16
SIDE = 4


def mm(a, b, dims):
    return lax.dot_general(a, b, dims, preferred_element_type=F32)


def sigmoid(z):
    return 0.5 * jnp.tanh(0.5 * z) + 0.5


def place():
    d, t = lax.axis_index("dp"), lax.axis_index("table")
    return d, t, d // SIDE, d % SIDE


def away(j):
    return TABLE // 2 + (1 - 2 * (j % 2)) * ((j + 1) // 2)


def table_peer(t, j):
    return (t + TABLE + away(j)) % TABLE


def table_source(t, j):
    return (t + 2 * TABLE - away(j)) % TABLE


def column(row):
    n = row.shape[1]
    tall = jnp.broadcast_to(row, (128, n)).T
    return jnp.concatenate([tall, tall], axis=1)

CHUNK = 2048


def scatter_block(hi, lo, g):
    k = g.shape[1]
    oht = jnp.where(lax.broadcasted_iota(I32, (256, k), 0) == lo, 1.0, 0.0).astype(BF16)
    hib = jnp.broadcast_to(hi.astype(F32).astype(BF16), (16, k))
    zero = jnp.zeros((16, k), BF16)
    lhs = jnp.concatenate([jnp.where(hib == jnp.array(q, BF16), g, zero) for q in range(32)], axis=0)
    return mm(lhs, oht, NT)


def lanes(i, size):
    return pl.ds(pl.multiple_of(i * size, size), size)


def turn_table(table_ref, rows_ref):
    w = 256
    n = rows_ref.shape[0]
    eye = jnp.where(lax.broadcasted_iota(I32, (w, w), 0) == lax.broadcasted_iota(I32, (w, w), 1), 1.0, 0.0).astype(BF16)

    def turn(b, c):
        block = jnp.concatenate([table_ref[:, pl.ds(pl.multiple_of(q * n + b * w, w), w)] for q in range(4)], axis=0)
        rows_ref[lanes(b, w), :] = mm(eye, block, NT)
        return c

    lax.fori_loop(0, n // w, turn, 0, unroll=2)


def gather_block(u, sid_ref, ids_ref, rows_ref, picked):
    n = rows_ref.shape[0]
    base = u * 256
    for r in range(256):
        picked[r : r + 1, :] = rows_ref[pl.ds(sid_ref[base + r] & (n - 1), 1), :]
    cols = picked[...].T
    q = jnp.broadcast_to(ids_ref[:, lanes(u, 256)] >> (n.bit_length() - 1), (32, 256))
    acc = cols[0:32]
    for i in range(1, 4):
        acc = jnp.where(q == i, cols[32 * i : 32 * i + 32], acc)
    return acc.astype(BF16)


def step_kernel(sid_ref, len_ref, ids_ref, table_ref, cot_ref, wh_ref, woh_ref, gin_ref, gmid_ref,
                out_ref, sum_ref,
                rows_ref, picked, stage, x_ref, c_ref, w_ref, wo_ref, p_ref, zd_ref, dz_ref, wt_ref, sd_ref, a_ref,
                o_ref, g_ref, idp_ref, ida_ref, idb_ref, home, ga, gb, acca, accb, sa, sb, ra, rb,
                wsem, esend, erecv, csend, crecv, isend, irecv, osend, orecv, gsend, grecv, asend, arecv, rsend, rrecv):
    d, t, xq, yq = place()

    def peers(q):
        return xq * SIDE + (yq + q) % SIDE, ((xq + q) % SIDE) * SIDE + yq

    weights = [pltpu.make_async_copy(wh_ref, w_ref, wsem.at[0]), pltpu.make_async_copy(woh_ref, wo_ref, wsem.at[1])]
    for c in weights:
        c.start()
    bar = pltpu.get_barrier_semaphore()

    def signal(j, c):
        pl.semaphore_signal(bar, inc=1, device_id=(d, table_peer(t, j)), device_id_type=MESH)
        return c

    lax.fori_loop(0, TABLE - 1, signal, 0)
    for q in range(1, SIDE):
        for peer in peers(q):
            pl.semaphore_signal(bar, inc=1, device_id=(peer, t), device_id_type=MESH)

    mine = lanes(t, 32)

    def remote(src, dst, send, recv, dev):
        return pltpu.make_async_remote_copy(
            src_ref=src, dst_ref=dst, send_sem=send, recv_sem=recv, device_id=dev, device_id_type=MESH)

    def emb_copy(j):
        return remote(stage.at[j], x_ref.at[mine, :], esend.at[j], erecv.at[j], (d, table_peer(t, j)))

    def cot_copy(j):
        u = table_peer(t, j)
        return remote(cot_ref.at[:, lanes(u, 256)], c_ref.at[mine, :], csend.at[j], crecv.at[j], (d, u))

    def id_copy(half, q):
        dst = ida_ref if half == 0 else idb_ref
        return remote(idp_ref, dst.at[q], isend.at[half, q], irecv.at[half, q], (peers(q)[half], t))

    turn_table(table_ref, rows_ref)

    def pick(j, c):
        stage[j] = gather_block(table_peer(t, j), sid_ref, ids_ref, rows_ref, picked)

        @pl.when(j == 0)
        def _():
            pl.semaphore_wait(bar, TABLE - 1 + 2 * (SIDE - 1))

        @pl.when(j < TABLE - 1)
        def _():
            emb_copy(j).start()

        return c

    lax.fori_loop(0, TABLE, pick, 0)
    lax.fori_loop(0, TABLE - 1, lambda j, c: (cot_copy(j).start(), c)[1], 0)

    def order(j, c):
        idp_ref[:, lanes((j + 1) % TABLE, 256)] = ids_ref[:, lanes(table_source(t, j), 256)]
        return c

    lax.fori_loop(0, TABLE, order, 0)
    x_ref[mine, :] = stage[TABLE - 1]
    c_ref[mine, :] = cot_ref[:, lanes(t, 256)]
    ida_ref[0] = idp_ref[...]
    idb_ref[0] = idp_ref[...]
    for half in range(2):
        for q in range(1, SIDE):
            id_copy(half, q).start()
    for c in weights:
        c.wait()
    lax.fori_loop(0, TABLE - 1, lambda j, c: (emb_copy(j).wait(), c)[1], 0)

    D, S = x_ref.shape
    hd = D // HEADS
    ln = len_ref[lax.axis_index("table")]
    x = x_ref[...].astype(F32)
    mu = jnp.mean(x, axis=0, keepdims=True)
    cen = x - mu
    r1 = lax.rsqrt(jnp.mean(cen * cen, axis=0, keepdims=True) + EPS)
    gin = column(gin_ref[...])
    gmid = column(gmid_ref[...])
    normed = (cen * r1 * gin).astype(BF16)
    for b in range(4):
        z = mm(w_ref[:, b * D:(b + 1) * D], normed, TN)
        sg = sigmoid(z)
        p_ref[b * D:(b + 1) * D, :] = (z * sg).astype(BF16)
        zd_ref[b * D:(b + 1) * D, :] = sg * (1.0 + z * (1.0 - sg))
    key_i = lax.broadcasted_iota(jnp.int32, (S, S), 0)
    qry_i = lax.broadcasted_iota(jnp.int32, (S, S), 1)
    inv = 1.0 / jnp.full((S, S), ln, jnp.int32).astype(F32)
    scale = jnp.where((key_i <= qry_i) & (key_i < ln), inv, 0.0)
    for h in range(HEADS):
        vT = p_ref[D + h * hd:D + (h + 1) * hd, :]
        qT = p_ref[2 * D + h * hd:2 * D + (h + 1) * hd, :]
        kT = p_ref[3 * D + h * hd:3 * D + (h + 1) * hd, :]
        s = mm(kT, qT, TN) * (hd ** -0.5)
        sg = sigmoid(s)
        wt = (s * sg * scale).astype(BF16)
        wt_ref[h] = wt
        sd_ref[h] = sg * (1.0 + s * (1.0 - sg)) * (scale * hd ** -0.5)
        a_ref[h * hd:(h + 1) * hd, :] = mm(vT, wt, NN)
    a = a_ref[...]
    cen2 = a - jnp.mean(a, axis=0, keepdims=True)
    r2 = lax.rsqrt(jnp.mean(cen2 * cen2, axis=0, keepdims=True) + EPS)
    nh2 = cen2 * r2
    u = p_ref[0:D, :].astype(F32)
    mixed = (nh2 * gmid * u).astype(BF16)
    o_ref[...] = (x_ref[...].astype(F32) + mm(wo_ref[...], mixed, TN)).astype(BF16)
    here = lanes(t, 256)

    def out_copy(j):
        u = table_peer(t, j)
        return remote(o_ref.at[lanes(u, 32), :], out_ref.at[:, here], osend.at[j], orecv.at[j], (d, u))

    lax.fori_loop(0, TABLE - 1, lambda j, c: (out_copy(j).start(), c)[1], 0)
    out_ref[:, here] = o_ref[mine, :]
    lax.fori_loop(0, TABLE - 1, lambda j, c: (cot_copy(j).wait(), c)[1], 0)

    pos = lax.broadcasted_iota(I32, (D, S), 1)
    g32 = jnp.where(pos < ln, c_ref[...].astype(F32), 0.0)
    g = g32.astype(BF16)
    dm = mm(wo_ref[...], g, NN).astype(BF16).astype(F32)
    dz_ref[0:D, :] = ((dm * nh2 * gmid).astype(BF16).astype(F32) * zd_ref[0:D, :]).astype(BF16)
    dn = dm * u * gmid
    da = r2 * (dn - jnp.mean(dn, axis=0, keepdims=True) - nh2 * jnp.mean(dn * nh2, axis=0, keepdims=True))
    a_ref[...] = da
    for h in range(HEADS):
        vT = p_ref[D + h * hd:D + (h + 1) * hd, :]
        qT = p_ref[2 * D + h * hd:2 * D + (h + 1) * hd, :]
        kT = p_ref[3 * D + h * hd:3 * D + (h + 1) * hd, :]
        dah = a_ref[h * hd:(h + 1) * hd, :].astype(BF16)
        wt = wt_ref[h]
        dw = mm(vT, dah, TN).astype(BF16).astype(F32)
        ds = (dw * sd_ref[h]).astype(BF16)
        for b, val in ((1, mm(dah, wt, NT)), (2, mm(kT, ds, NN)), (3, mm(qT, ds, NT))):
            rows = slice(b * D + h * hd, b * D + (h + 1) * hd)
            dz_ref[rows, :] = (val.astype(BF16).astype(F32) * zd_ref[rows, :]).astype(BF16)
    dnr = mm(w_ref[...], dz_ref[...], NN).astype(BF16).astype(F32) * gin
    x = x_ref[...].astype(F32)
    nh1 = (x - mu) * r1
    de = r1 * (dnr - jnp.mean(dnr, axis=0, keepdims=True) - nh1 * jnp.mean(dnr * nh1, axis=0, keepdims=True))
    g_ref[...] = (de + g32).astype(BF16)


    def grad_copy(j):
        u = table_peer(t, j)
        return remote(g_ref.at[lanes(u, 32), :], home.at[:, lanes((j + 1) % TABLE, 256)], gsend.at[j], grecv.at[j], (d, u))

    lax.fori_loop(0, TABLE - 1, lambda j, c: (grad_copy(j).start(), c)[1], 0)
    home[:, 0:256] = g_ref[mine, :]
    acca[...] = jnp.zeros_like(acca)
    accb[...] = jnp.zeros_like(accb)
    for half in range(2):
        for q in range(1, SIDE):
            id_copy(half, q).wait()

    def row_copy(half, q, n):
        at = lanes(n, CHUNK)
        src, dst = (home.at[0:16, at], ga) if half == 0 else (home.at[16:32, at], gb)
        return remote(src, dst.at[q, :, at], asend.at[half, q, n], arecv.at[half, q, n], (peers(q)[half], t))

    per = CHUNK // 256

    def add(i, c):
        n, q = i // SIDE, i % SIDE
        at = lanes(n, CHUNK)

        @pl.when(q == 0)
        def _():
            lax.fori_loop(jnp.maximum(n * per - 1, 0), n * per + per - 1, lambda j, e: (grad_copy(j).wait(), e)[1], 0)
            for r in range(1, SIDE):
                row_copy(0, r, n).start()
                row_copy(1, r, n).start()
            ga[0, :, at] = home[0:16, at]
            gb[0, :, at] = home[16:32, at]

        @pl.when(q > 0)
        def _():
            row_copy(0, q, n).wait()
            row_copy(1, q, n).wait()

        ids = ida_ref[q, :, at]
        hi = jnp.where(((ids >> 11) & 3) == yq, (ids >> 13) * 8 + ((ids >> 8) & 7), -1)
        acca[...] += scatter_block(hi, ids & 255, ga[q, :, at])
        ids = idb_ref[q, :, at]
        hi = jnp.where((ids >> 13) == xq, (ids >> 8) & 31, -1)
        accb[...] += scatter_block(hi, ids & 255, gb[q, :, at])
        return c

    lax.fori_loop(0, SIDE * (home.shape[1] // CHUNK), add, 0)
    sa[...] = acca[...].astype(BF16)
    sb[...] = accb[...].astype(BF16)

    def sum_copy(half, q):
        to, send, recv = ((xq + q) % SIDE, sa, ra) if half == 0 else ((yq + q) % SIDE, sb, rb)
        return remote(send.at[lanes(to, 128), :], recv.at[q], rsend.at[half, q], rrecv.at[half, q], (peers(q)[1 - half], t))

    for q in range(1, SIDE):
        for half in range(2):
            sum_copy(half, q).start()
    lax.fori_loop(0, TABLE - 1, lambda j, c: (out_copy(j).wait(), c)[1], 0)
    for half, acc, recv, own in ((0, acca, ra, xq), (1, accb, rb, yq)):
        total = acc[lanes(own, 128), :]
        for q in range(1, SIDE):
            sum_copy(half, q).wait()
            total = total + recv[q].astype(F32)
        for h in range(8):
            sum_ref[half * 16 : half * 16 + 16, h * 256 : (h + 1) * 256] = total[h * 16 : (h + 1) * 16]


def on_device(item_ids, user_len, emb_table, cotangent, w_uvqk, w_out, gain_in, gain_mid):
    f, n = cotangent.shape
    vocab = emb_table.shape[1]
    D, S = TABLE * f, n // TABLE
    sem = pltpu.SemaphoreType.DMA
    ANY = pl.BlockSpec(memory_space=pl.ANY)
    V = pltpu.VMEM
    return pl.pallas_call(
        step_kernel,
        out_shape=(jax.ShapeDtypeStruct((f, n), BF16), jax.ShapeDtypeStruct((f, vocab // lax.axis_size("dp")), F32)),
        in_specs=[SM, SM, VM, VM, VM, ANY, ANY, VM, VM],
        out_specs=(VM, VM),
        scratch_shapes=[
            V((vocab // 4, 4 * f), F32), V((S, 4 * f), F32), V((TABLE, f, S), BF16), V((D, S), BF16), V((D, S), BF16),
            V((D, 4 * D), BF16), V((D, D), BF16), V((4 * D, S), BF16), V((4 * D, S), F32), V((4 * D, S), BF16),
            V((HEADS, S, S), BF16), V((HEADS, S, S), F32), V((D, S), F32), V((D, S), BF16), V((D, S), BF16),
            V((1, n), I32), V((SIDE, 1, n), I32), V((SIDE, 1, n), I32), V((f, n), BF16),
            V((SIDE, 16, n), BF16), V((SIDE, 16, n), BF16), V((512, 256), F32), V((512, 256), F32),
            V((512, 256), BF16), V((512, 256), BF16), V((SIDE, 128, 256), BF16), V((SIDE, 128, 256), BF16), sem((2,)),
        ]
        + [sem((TABLE,))] * 4 + [sem((2, SIDE))] * 2 + [sem((TABLE,))] * 4
        + [sem((2, SIDE, n // CHUNK))] * 2 + [sem((2, SIDE))] * 2,
        compiler_params=pltpu.CompilerParams(collective_id=0, has_side_effects=True, vmem_limit_bytes=48 << 20),
    )(item_ids, user_len, item_ids.reshape(1, n), emb_table, cotangent, w_uvqk, w_out,
      gain_in.reshape(1, D), gain_mid.reshape(1, D))


def solution(mesh):
    return jax.shard_map(
        on_device,
        mesh=mesh,
        in_specs=(P("dp"), P("dp"), P("table", None), P("table", "dp"), P(), P(), P(), P()),
        out_specs=(P("table", "dp"), P("table", "dp")),
        check_vma=False,
    )
```

```python
import functools

import jax
import jax.numpy as jnp
from jax import lax
from jax.experimental import pallas as pl
from jax.experimental.pallas import tpu as pltpu
from jax.sharding import PartitionSpec as P

F32, BF16, I32 = jnp.float32, jnp.bfloat16, jnp.int32
MESH = pl.DeviceIdType.MESH
VM = pl.BlockSpec(memory_space=pltpu.VMEM)
SM = pl.BlockSpec(memory_space=pltpu.SMEM)
EPS = 1e-5
HEADS = 8
NN = (((1,), (0,)), ((), ()))
TN = (((0,), (0,)), ((), ()))
NT = (((1,), (1,)), ((), ()))
TABLE = 16
SIDE = 4


def mm(a, b, dims):
    return lax.dot_general(a, b, dims, preferred_element_type=F32)


def sigmoid(z):
    return 0.5 * jnp.tanh(0.5 * z) + 0.5


def place():
    d, t = lax.axis_index("dp"), lax.axis_index("table")
    return d, t, d // SIDE, d % SIDE


def away(j):
    return TABLE // 2 + (1 - 2 * (j % 2)) * ((j + 1) // 2)


def table_peer(t, j):
    return (t + TABLE + away(j)) % TABLE


def table_source(t, j):
    return (t + 2 * TABLE - away(j)) % TABLE


def column(row):
    n = row.shape[1]
    tall = jnp.broadcast_to(row, (128, n)).T
    return jnp.concatenate([tall, tall], axis=1)

CHUNK = 1024


def scatter_block(hi, lo, g):
    k = g.shape[1]
    low = jnp.broadcast_to(lo.astype(F32).astype(BF16), (256, k))
    row = lax.broadcasted_iota(I32, (256, k), 0).astype(F32).astype(BF16)
    oht = jnp.where(row == low, jnp.ones((256, k), BF16), jnp.zeros((256, k), BF16))
    hib = jnp.broadcast_to(hi.astype(F32).astype(BF16), (16, k))
    zero = jnp.zeros((16, k), BF16)
    lhs = jnp.concatenate([jnp.where(hib == jnp.array(q, BF16), g, zero) for q in range(32)], axis=0)
    return mm(lhs, oht, NT)


PIECE = 2048
AHEAD = 1
VMEM_LIMIT = 60 << 20


def lanes(i, size):
    return pl.ds(pl.multiple_of(i * size, size), size)


def turn_table(table_ref, rows_ref, first, blocks):
    w = 256
    n = rows_ref.shape[0]

    def turn(b, c):
        block = jnp.concatenate(
            [table_ref[:, pl.ds(pl.multiple_of(q * n + b * w, w), w)].astype(F32) for q in range(4)], axis=0
        )
        rows_ref[lanes(b, w), :] = block.T
        return c

    lax.fori_loop(first, first + blocks, turn, 0, unroll=4)


def gather_block(u, sid_ref, ids_ref, rows_ref, picked):
    n = rows_ref.shape[0]
    base = u * 256
    for r in range(256):
        picked[r : r + 1, :] = rows_ref[pl.ds(sid_ref[base + r] & (n - 1), 1), :]
    cols = picked[...].T
    q = jnp.broadcast_to(ids_ref[:, lanes(u, 256)] >> (n.bit_length() - 1), (32, 256))
    acc = cols[0:32]
    for i in range(1, 4):
        acc = jnp.where(q == i, cols[32 * i : 32 * i + 32], acc)
    return acc.astype(BF16)


def step_kernel(sidh_ref, lenh_ref, idsh_ref, tableh_ref, cot_ref, wh_ref, woh_ref, ginh_ref, gmidh_ref,
                out_ref, sum_ref,
                sid_ref, len_ref, ids_ref, gin_ref, gmid_ref, table_ref, rows_ref, picked, stage, x_ref, c_ref, w_ref, wo_ref, p_ref, zd_ref, dz_ref, wt_ref, sd_ref, a_ref,
                o_ref, g_ref, idp_ref, ida_ref, idb_ref, home, ga, gb, acca, accb, sa, sb, ra, rb,
                wsem, tsem, ssem, esend, erecv, csend, crecv, isend, irecv, osend, orecv, gsend, grecv, asend, arecv, rsend, rrecv):
    d, t, xq, yq = place()

    def peers(q):
        return xq * SIDE + (yq + q) % SIDE, ((xq + q) % SIDE) * SIDE + yq

    weights = [pltpu.make_async_copy(wh_ref, w_ref, wsem.at[0]), pltpu.make_async_copy(woh_ref, wo_ref, wsem.at[1])]
    def piece(c, q):
        at = pl.ds(pl.multiple_of(q * rows_ref.shape[0] + c * PIECE, PIECE), PIECE)
        return pltpu.make_async_copy(tableh_ref.at[:, at], table_ref.at[:, at], tsem.at[c, q])

    small = [pltpu.make_async_copy(a, b, ssem.at[i]) for i, (a, b) in enumerate(
        ((sidh_ref, sid_ref), (idsh_ref, ids_ref), (lenh_ref, len_ref), (ginh_ref, gin_ref), (gmidh_ref, gmid_ref)))]
    pieces = rows_ref.shape[0] // PIECE
    for c in range(pieces):
        for q in range(4):
            piece(c, q).start()
        if c == 0:
            for a in small:
                a.start()
    own_cot = pltpu.make_async_copy(cot_ref.at[:, lanes(t, 256)], c_ref.at[lanes(t, 32), :], wsem.at[2])
    own_cot.start()
    for c in weights:
        c.start()
    bar = pltpu.get_barrier_semaphore()

    def signal(j, c):
        pl.semaphore_signal(bar, inc=1, device_id=(d, table_peer(t, j)), device_id_type=MESH)
        return c

    lax.fori_loop(0, TABLE - 1, signal, 0)
    for q in range(1, SIDE):
        for peer in peers(q):
            pl.semaphore_signal(bar, inc=1, device_id=(peer, t), device_id_type=MESH)

    mine = lanes(t, 32)

    def remote(src, dst, send, recv, dev):
        return pltpu.make_async_remote_copy(
            src_ref=src, dst_ref=dst, send_sem=send, recv_sem=recv, device_id=dev, device_id_type=MESH)

    def emb_copy(j):
        return remote(stage.at[j], x_ref.at[mine, :], esend.at[j], erecv.at[j], (d, table_peer(t, j)))

    def cot_copy(j):
        u = table_peer(t, j)
        return remote(cot_ref.at[:, lanes(u, 256)], c_ref.at[mine, :], csend.at[j], crecv.at[j], (d, u))

    def id_copy(half, q):
        dst = ida_ref if half == 0 else idb_ref
        return remote(idp_ref, dst.at[q], isend.at[half, q], irecv.at[half, q], (peers(q)[half], t))

    for c in range(pieces):
        for q in range(4):
            piece(c, q).wait()
        turn_table(table_ref, rows_ref, c * (PIECE // 256), PIECE // 256)
    for c in small[:2]:
        c.wait()

    def pick(j, c):
        stage[j] = gather_block(table_peer(t, j), sid_ref, ids_ref, rows_ref, picked)

        @pl.when(j == AHEAD - 1)
        def _():
            pl.semaphore_wait(bar, TABLE - 1 + 2 * (SIDE - 1))
            lax.fori_loop(0, AHEAD, lambda k, e: (emb_copy(k).start(), e)[1], 0)

        @pl.when((j >= AHEAD) & (j < TABLE - 1))
        def _():
            emb_copy(j).start()

        return c

    lax.fori_loop(0, TABLE, pick, 0)
    lax.fori_loop(0, TABLE - 1, lambda j, c: (cot_copy(j).start(), c)[1], 0)

    def order(j, c):
        idp_ref[:, lanes(TABLE - 1 - j, 256)] = ids_ref[:, lanes(table_source(t, j), 256)]
        return c

    lax.fori_loop(0, TABLE, order, 0)
    x_ref[mine, :] = stage[TABLE - 1]
    ida_ref[0] = idp_ref[...]
    idb_ref[0] = idp_ref[...]
    for half in range(2):
        for q in range(1, SIDE):
            id_copy(half, q).start()
    for c in weights + small[2:]:
        c.wait()
    lax.fori_loop(0, TABLE - 1, lambda j, c: (emb_copy(j).wait(), c)[1], 0)

    D, S = x_ref.shape
    hd = D // HEADS
    ln = len_ref[lax.axis_index("table")]
    x = x_ref[...].astype(F32)
    mu = jnp.mean(x, axis=0, keepdims=True)
    cen = x - mu
    r1 = lax.rsqrt(jnp.mean(cen * cen, axis=0, keepdims=True) + EPS)
    gin = column(gin_ref[...])
    gmid = column(gmid_ref[...])
    normed = (cen * r1 * gin).astype(BF16)
    for b in range(4):
        z = mm(w_ref[:, b * D:(b + 1) * D], normed, TN)
        sg = sigmoid(z)
        p_ref[b * D:(b + 1) * D, :] = (z * sg).astype(BF16)
        zd_ref[b * D:(b + 1) * D, :] = sg * (1.0 + z * (1.0 - sg))
    key_i = lax.broadcasted_iota(jnp.int32, (S, S), 0)
    qry_i = lax.broadcasted_iota(jnp.int32, (S, S), 1)
    inv = 1.0 / jnp.full((S, S), ln, jnp.int32).astype(F32)
    scale = jnp.where((key_i <= qry_i) & (key_i < ln), inv, 0.0)
    for h in range(HEADS):
        vT = p_ref[D + h * hd:D + (h + 1) * hd, :]
        qT = p_ref[2 * D + h * hd:2 * D + (h + 1) * hd, :]
        kT = p_ref[3 * D + h * hd:3 * D + (h + 1) * hd, :]
        s = mm(kT, qT, TN) * (hd ** -0.5)
        sg = sigmoid(s)
        wt = (s * sg * scale).astype(BF16)
        wt_ref[h] = wt
        sd_ref[h] = sg * (1.0 + s * (1.0 - sg)) * (scale * hd ** -0.5)
        a_ref[h * hd:(h + 1) * hd, :] = mm(vT, wt, NN)
    a = a_ref[...]
    cen2 = a - jnp.mean(a, axis=0, keepdims=True)
    r2 = lax.rsqrt(jnp.mean(cen2 * cen2, axis=0, keepdims=True) + EPS)
    nh2 = cen2 * r2
    u = p_ref[0:D, :].astype(F32)
    mixed = (nh2 * gmid * u).astype(BF16)
    o_ref[...] = (x_ref[...].astype(F32) + mm(wo_ref[...], mixed, TN)).astype(BF16)
    here = lanes(t, 256)

    def out_copy(j):
        u = table_peer(t, j)
        return remote(o_ref.at[lanes(u, 32), :], out_ref.at[:, here], osend.at[j], orecv.at[j], (d, u))

    lax.fori_loop(0, TABLE - 1, lambda j, c: (out_copy(j).start(), c)[1], 0)
    out_ref[:, here] = o_ref[mine, :]
    lax.fori_loop(0, TABLE - 1, lambda j, c: (cot_copy(j).wait(), c)[1], 0)

    own_cot.wait()
    pos = lax.broadcasted_iota(I32, (D, S), 1)
    g32 = jnp.where(pos < ln, c_ref[...].astype(F32), 0.0)
    g = g32.astype(BF16)
    dm = mm(wo_ref[...], g, NN).astype(BF16).astype(F32)
    dz_ref[0:D, :] = ((dm * nh2 * gmid).astype(BF16).astype(F32) * zd_ref[0:D, :]).astype(BF16)
    dn = dm * u * gmid
    da = r2 * (dn - jnp.mean(dn, axis=0, keepdims=True) - nh2 * jnp.mean(dn * nh2, axis=0, keepdims=True))
    a_ref[...] = da
    for h in range(HEADS):
        vT = p_ref[D + h * hd:D + (h + 1) * hd, :]
        qT = p_ref[2 * D + h * hd:2 * D + (h + 1) * hd, :]
        kT = p_ref[3 * D + h * hd:3 * D + (h + 1) * hd, :]
        dah = a_ref[h * hd:(h + 1) * hd, :].astype(BF16)
        wt = wt_ref[h]
        dw = mm(vT, dah, TN).astype(BF16).astype(F32)
        ds = (dw * sd_ref[h]).astype(BF16)
        for b, val in ((1, mm(dah, wt, NT)), (2, mm(kT, ds, NN)), (3, mm(qT, ds, NT))):
            rows = slice(b * D + h * hd, b * D + (h + 1) * hd)
            dz_ref[rows, :] = (val.astype(BF16).astype(F32) * zd_ref[rows, :]).astype(BF16)
    dnr = mm(w_ref[...], dz_ref[...], NN).astype(BF16).astype(F32) * gin
    x = x_ref[...].astype(F32)
    nh1 = (x - mu) * r1
    de = r1 * (dnr - jnp.mean(dnr, axis=0, keepdims=True) - nh1 * jnp.mean(dnr * nh1, axis=0, keepdims=True))
    g_ref[...] = (de + g32).astype(BF16)


    def grad_copy(j):
        u = table_peer(t, j)
        return remote(g_ref.at[lanes(u, 32), :], home.at[:, lanes(TABLE - 1 - j, 256)], gsend.at[j], grecv.at[j], (d, u))

    lax.fori_loop(1, TABLE, lambda k, c: (grad_copy(TABLE - 1 - k).start(), c)[1], 0)
    home[:, 0:256] = g_ref[mine, :]
    for half in range(2):
        for q in range(1, SIDE):
            id_copy(half, q).wait()

    def row_copy(half, q, n):
        at = lanes(n, CHUNK)
        src, dst = (home.at[0:16, at], ga) if half == 0 else (home.at[16:32, at], gb)
        return remote(src, dst.at[q, :, at], asend.at[half, q, n], arecv.at[half, q, n], (peers(q)[half], t))

    per = CHUNK // 256

    def both(qs, at, xa, xb, start):
        ids = jnp.concatenate([ida_ref[q, :, at] for q in qs], axis=1)
        hi = jnp.where(((ids >> 11) & 3) == yq, (ids >> 13) * 8 + ((ids >> 8) & 7), -1)
        va = scatter_block(hi, ids & 255, xa)
        ids = jnp.concatenate([idb_ref[q, :, at] for q in qs], axis=1)
        hi = jnp.where((ids >> 13) == xq, (ids >> 8) & 31, -1)
        vb = scatter_block(hi, ids & 255, xb)
        acca[...] = va if start else acca[...] + va
        accb[...] = vb if start else accb[...] + vb

    chunks = home.shape[1] // CHUNK
    others = range(1, SIDE)

    def own(n, start):
        at = lanes(n, CHUNK)
        lax.fori_loop(jnp.maximum(n * per, 1), n * per + per, lambda k, e: (grad_copy(TABLE - 1 - k).wait(), e)[1], 0)
        for r in others:
            row_copy(0, r, n).start()
            row_copy(1, r, n).start()
        both((0,), at, home[0:16, at], home[16:32, at], start)

    def rest(n):
        at = lanes(n, CHUNK)
        for r in others:
            row_copy(0, r, n).wait()
            row_copy(1, r, n).wait()
        both(others, at, jnp.concatenate([ga[q, :, at] for q in others], axis=1),
             jnp.concatenate([gb[q, :, at] for q in others], axis=1), False)

    def add(n, c):
        own(n, False)
        rest(n - 1)
        return c

    own(0, True)
    lax.fori_loop(1, chunks, add, 0)
    rest(chunks - 1)
    sa[...] = acca[...].astype(BF16)
    sb[...] = accb[...].astype(BF16)

    def sum_copy(half, q):
        to, send, recv = ((xq + q) % SIDE, sa, ra) if half == 0 else ((yq + q) % SIDE, sb, rb)
        return remote(send.at[lanes(to, 128), :], recv.at[q], rsend.at[half, q], rrecv.at[half, q], (peers(q)[1 - half], t))

    for q in range(1, SIDE):
        for half in range(2):
            sum_copy(half, q).start()
    lax.fori_loop(0, TABLE - 1, lambda j, c: (out_copy(j).wait(), c)[1], 0)
    for half, acc, recv, own in ((0, acca, ra, xq), (1, accb, rb, yq)):
        total = acc[lanes(own, 128), :]
        for q in range(1, SIDE):
            sum_copy(half, q).wait()
            total = total + recv[q].astype(F32)
        for h in range(8):
            sum_ref[half * 16 : half * 16 + 16, h * 256 : (h + 1) * 256] = total[h * 16 : (h + 1) * 16]


def finish_kernel(out_ref, sum_ref, out_end, sum_end, out_buf, sum_buf, sems):
    moves = []
    for k in range(2):
        for a, (src, buf, dst) in enumerate(((out_ref, out_buf, out_end), (sum_ref, sum_buf, sum_end))):
            at = pl.ds(k * (src.shape[0] // 2), src.shape[0] // 2)
            moves.append((pltpu.make_async_copy(src.at[at], buf.at[at], sems.at[0, a, k]),
                          pltpu.make_async_copy(buf.at[at], dst.at[at], sems.at[1, a, k])))
    for into, _ in moves:
        into.start()
    for into, back in moves:
        into.wait()
        back.start()
    for _, back in moves:
        back.wait()


def finish(out, total):
    HB = pl.BlockSpec(memory_space=pltpu.HBM)
    return pl.pallas_call(
        finish_kernel,
        out_shape=tuple(jax.ShapeDtypeStruct(a.shape, a.dtype) for a in (out, total)),
        in_specs=[HB] * 2,
        out_specs=(HB, HB),
        scratch_shapes=[pltpu.VMEM(out.shape, out.dtype), pltpu.VMEM(total.shape, total.dtype),
                        pltpu.SemaphoreType.DMA((2, 2, 2))],
    )(out, total)


def on_device(item_ids, user_len, emb_table, cotangent, w_uvqk, w_out, gain_in, gain_mid):
    f, n = cotangent.shape
    vocab = emb_table.shape[1]
    D, S = TABLE * f, n // TABLE
    sem = pltpu.SemaphoreType.DMA
    HB = pl.BlockSpec(memory_space=pltpu.HBM)
    V = pltpu.VMEM
    return finish(*pl.pallas_call(
        step_kernel,
        out_shape=(jax.ShapeDtypeStruct((f, n), BF16), jax.ShapeDtypeStruct((f, vocab // lax.axis_size("dp")), F32)),
        in_specs=[HB] * 9,
        out_specs=(VM, VM),
        scratch_shapes=[
            pltpu.SMEM((n,), I32), pltpu.SMEM(user_len.shape, I32), V((1, n), I32), V((1, D), F32), V((1, D), F32),
            V((f, vocab), BF16), V((vocab // 4, 4 * f), F32), V((S, 4 * f), F32), V((TABLE, f, S), BF16), V((D, S), BF16), V((D, S), BF16),
            V((D, 4 * D), BF16), V((D, D), BF16), V((4 * D, S), BF16), V((4 * D, S), F32), V((4 * D, S), BF16),
            V((HEADS, S, S), BF16), V((HEADS, S, S), F32), V((D, S), F32), V((D, S), BF16), V((D, S), BF16),
            V((1, n), I32), V((SIDE, 1, n), I32), V((SIDE, 1, n), I32), V((f, n), BF16),
            V((SIDE, 16, n), BF16), V((SIDE, 16, n), BF16), V((512, 256), F32), V((512, 256), F32),
            V((512, 256), BF16), V((512, 256), BF16), V((SIDE, 128, 256), BF16), V((SIDE, 128, 256), BF16), sem((3,)),
            sem((vocab // 4 // PIECE, 4)), sem((5,)),
        ]
        + [sem((TABLE,))] * 4 + [sem((2, SIDE))] * 2 + [sem((TABLE,))] * 4
        + [sem((2, SIDE, n // CHUNK))] * 2 + [sem((2, SIDE))] * 2,
        compiler_params=pltpu.CompilerParams(collective_id=0, has_side_effects=True, vmem_limit_bytes=VMEM_LIMIT),
    )(item_ids, user_len, item_ids.reshape(1, n), emb_table, cotangent, w_uvqk, w_out,
      gain_in.reshape(1, D), gain_mid.reshape(1, D)))


def solution(mesh):
    return jax.shard_map(
        on_device,
        mesh=mesh,
        in_specs=(P("dp"), P("dp"), P("table", None), P("table", "dp"), P(), P(), P(), P()),
        out_specs=(P("table", "dp"), P("table", "dp")),
        check_vma=False,
    )
```

```python
import functools

import jax
import jax.numpy as jnp
from jax import lax
from jax.experimental import pallas as pl
from jax.experimental.pallas import tpu as pltpu
from jax.sharding import PartitionSpec as P

F32, BF16, I32 = jnp.float32, jnp.bfloat16, jnp.int32
MESH = pl.DeviceIdType.MESH
VM = pl.BlockSpec(memory_space=pltpu.VMEM)
SM = pl.BlockSpec(memory_space=pltpu.SMEM)
EPS = 1e-5
HEADS = 8
NN = (((1,), (0,)), ((), ()))
TN = (((0,), (0,)), ((), ()))
NT = (((1,), (1,)), ((), ()))
TABLE = 16
SIDE = 4


def mm(a, b, dims):
    return lax.dot_general(a, b, dims, preferred_element_type=F32)


def sigmoid(z):
    return 0.5 * jnp.tanh(0.5 * z) + 0.5


def place():
    d, t = lax.axis_index("dp"), lax.axis_index("table")
    return d, t, d // SIDE, d % SIDE


def away(j):
    return TABLE // 2 + (1 - 2 * (j % 2)) * ((j + 1) // 2)


def table_peer(t, j):
    return (t + TABLE + away(j)) % TABLE


def table_source(t, j):
    return (t + 2 * TABLE - away(j)) % TABLE


def column(row):
    n = row.shape[1]
    tall = jnp.broadcast_to(row, (128, n)).T
    return jnp.concatenate([tall, tall], axis=1)

CHUNK = 1024


def low_bits(lo):
    k = lo.shape[1]
    low = jnp.broadcast_to(lo.astype(F32).astype(BF16), (256, k))
    row = lax.broadcasted_iota(I32, (256, k), 0).astype(F32).astype(BF16)
    return jnp.where(row == low, jnp.ones((256, k), BF16), jnp.zeros((256, k), BF16))


def scatter_block(hi, oht, g, parts):
    k = g.shape[1]
    hib = jnp.broadcast_to(hi.astype(F32).astype(BF16), (16, k))
    zero = jnp.zeros((16, k), BF16)
    lhs = [jnp.where(hib == jnp.array(8 * p + q, BF16), g, zero) for p in parts for q in range(8)]
    return mm(jnp.concatenate(lhs, axis=0), oht, NT)


PIECE = 2048
VMEM_LIMIT = 60 << 20


def lanes(i, size):
    return pl.ds(pl.multiple_of(i * size, size), size)


def turn_table(table_ref, rows_ref, first, blocks):
    w = 256
    n = rows_ref.shape[0]

    def turn(b, c):
        block = jnp.concatenate(
            [table_ref[:, pl.ds(pl.multiple_of(q * n + b * w, w), w)].astype(F32) for q in range(4)], axis=0
        )
        rows_ref[lanes(b, w), :] = block.T
        return c

    lax.fori_loop(first, first + blocks, turn, 0, unroll=4)


def gather_block(u, sid_ref, ids_ref, rows_ref, picked):
    n = rows_ref.shape[0]
    base = u * 256
    for r in range(256):
        picked[r : r + 1, :] = rows_ref[pl.ds(sid_ref[base + r] & (n - 1), 1), :]
    cols = picked[...].T
    q = jnp.broadcast_to(ids_ref[:, lanes(u, 256)] >> (n.bit_length() - 1), (32, 256))
    acc = cols[0:32]
    for i in range(1, 4):
        acc = jnp.where(q == i, cols[32 * i : 32 * i + 32], acc)
    return acc.astype(BF16)


def step_kernel(sidh_ref, lenh_ref, idsh_ref, tableh_ref, cot_ref, wh_ref, woh_ref, ginh_ref, gmidh_ref,
                out_ref, sum_ref,
                sid_ref, len_ref, ids_ref, gin_ref, gmid_ref, table_ref, rows_ref, picked, stage, x_ref, c_ref, w_ref, wo_ref, p_ref, zd_ref, dz_ref, wt_ref, sd_ref, a_ref,
                o_ref, g_ref, idp_ref, ida_ref, idb_ref, home, ga, gb, acca, accb, sa, sb, ra, rb,
                wsem, tsem, ssem, esend, erecv, csend, crecv, isend, irecv, osend, orecv, gsend, grecv, asend, arecv, rsend, rrecv):
    d, t, xq, yq = place()

    def peers(q):
        return xq * SIDE + (yq + q) % SIDE, ((xq + q) % SIDE) * SIDE + yq

    weights = [pltpu.make_async_copy(wh_ref, w_ref, wsem.at[0]), pltpu.make_async_copy(woh_ref, wo_ref, wsem.at[1])]
    def piece(c, q):
        at = pl.ds(pl.multiple_of(q * rows_ref.shape[0] + c * PIECE, PIECE), PIECE)
        return pltpu.make_async_copy(tableh_ref.at[:, at], table_ref.at[:, at], tsem.at[c, q])

    small = [pltpu.make_async_copy(a, b, ssem.at[i]) for i, (a, b) in enumerate(
        ((sidh_ref, sid_ref), (idsh_ref, ids_ref), (lenh_ref, len_ref), (ginh_ref, gin_ref), (gmidh_ref, gmid_ref)))]
    pieces = rows_ref.shape[0] // PIECE
    for c in range(pieces):
        for q in range(4):
            piece(c, q).start()
        if c == 0:
            for a in small:
                a.start()
    own_cot = pltpu.make_async_copy(cot_ref.at[:, lanes(t, 256)], c_ref.at[lanes(t, 32), :], wsem.at[2])
    own_cot.start()
    for c in weights:
        c.start()
    bar = pltpu.get_barrier_semaphore()

    def signal(j, c):
        pl.semaphore_signal(bar, inc=1, device_id=(d, table_peer(t, j)), device_id_type=MESH)
        return c

    lax.fori_loop(0, TABLE - 1, signal, 0)
    for q in range(1, SIDE):
        for peer in peers(q):
            pl.semaphore_signal(bar, inc=1, device_id=(peer, t), device_id_type=MESH)

    mine = lanes(t, 32)

    def remote(src, dst, send, recv, dev):
        return pltpu.make_async_remote_copy(
            src_ref=src, dst_ref=dst, send_sem=send, recv_sem=recv, device_id=dev, device_id_type=MESH)

    def emb_copy(j):
        return remote(stage.at[j], x_ref.at[mine, :], esend.at[j], erecv.at[j], (d, table_peer(t, j)))

    def cot_copy(j):
        u = table_peer(t, j)
        return remote(cot_ref.at[:, lanes(u, 256)], c_ref.at[mine, :], csend.at[j], crecv.at[j], (d, u))

    def id_copy(half, q):
        dst = ida_ref if half == 0 else idb_ref
        return remote(idp_ref, dst.at[q], isend.at[half, q], irecv.at[half, q], (peers(q)[half], t))

    for c in range(pieces):
        for q in range(4):
            piece(c, q).wait()
        turn_table(table_ref, rows_ref, c * (PIECE // 256), PIECE // 256)
    for c in small[:2]:
        c.wait()

    def pick(i, c):
        blocks = [gather_block(table_peer(t, 2 * i + k), sid_ref, ids_ref, rows_ref, picked.at[k]) for k in range(2)]
        for k in range(2):
            stage[2 * i + k] = blocks[k]

        @pl.when(i == 0)
        def _():
            pl.semaphore_wait(bar, TABLE - 1 + 2 * (SIDE - 1))

        emb_copy(2 * i).start()

        @pl.when(i < TABLE // 2 - 1)
        def _():
            emb_copy(2 * i + 1).start()

        return c

    lax.fori_loop(0, TABLE // 2, pick, 0)
    lax.fori_loop(0, TABLE - 1, lambda j, c: (cot_copy(j).start(), c)[1], 0)

    def order(j, c):
        idp_ref[:, lanes(TABLE - 1 - j, 256)] = ids_ref[:, lanes(table_source(t, j), 256)]
        return c

    lax.fori_loop(0, TABLE, order, 0)
    x_ref[mine, :] = stage[TABLE - 1]
    ida_ref[0] = idp_ref[...]
    idb_ref[0] = idp_ref[...]
    for half in range(2):
        for q in range(1, SIDE):
            id_copy(half, q).start()
    for c in weights + small[2:]:
        c.wait()
    D, S = x_ref.shape
    hd = D // HEADS
    ln = len_ref[lax.axis_index("table")]
    gin = column(gin_ref[...])
    gmid = column(gmid_ref[...])
    key_i = lax.broadcasted_iota(jnp.int32, (S, S), 0)
    qry_i = lax.broadcasted_iota(jnp.int32, (S, S), 1)
    inv = 1.0 / jnp.full((S, S), ln, jnp.int32).astype(F32)
    scale = jnp.where((key_i <= qry_i) & (key_i < ln), inv, 0.0)
    lax.fori_loop(0, TABLE - 1, lambda j, c: (emb_copy(j).wait(), c)[1], 0)

    x = x_ref[...].astype(F32)
    mu = jnp.mean(x, axis=0, keepdims=True)
    cen = x - mu
    r1 = lax.rsqrt(jnp.mean(cen * cen, axis=0, keepdims=True) + EPS)
    normed = (cen * r1 * gin).astype(BF16)
    for b in range(4):
        z = mm(w_ref[:, b * D:(b + 1) * D], normed, TN)
        sg = sigmoid(z)
        p_ref[b * D:(b + 1) * D, :] = (z * sg).astype(BF16)
        zd_ref[b * D:(b + 1) * D, :] = sg * (1.0 + z * (1.0 - sg))
    for h in range(HEADS):
        vT = p_ref[D + h * hd:D + (h + 1) * hd, :]
        qT = p_ref[2 * D + h * hd:2 * D + (h + 1) * hd, :]
        kT = p_ref[3 * D + h * hd:3 * D + (h + 1) * hd, :]
        s = mm(kT, qT, TN) * (hd ** -0.5)
        sg = sigmoid(s)
        wt = (s * sg * scale).astype(BF16)
        wt_ref[h] = wt
        sd_ref[h] = sg * (1.0 + s * (1.0 - sg)) * (scale * hd ** -0.5)
        a_ref[h * hd:(h + 1) * hd, :] = mm(vT, wt, NN)
    a = a_ref[...]
    cen2 = a - jnp.mean(a, axis=0, keepdims=True)
    r2 = lax.rsqrt(jnp.mean(cen2 * cen2, axis=0, keepdims=True) + EPS)
    nh2 = cen2 * r2
    u = p_ref[0:D, :].astype(F32)
    mixed = (nh2 * gmid * u).astype(BF16)
    o_ref[...] = (x_ref[...].astype(F32) + mm(wo_ref[...], mixed, TN)).astype(BF16)
    here = lanes(t, 256)

    def out_copy(j):
        u = table_peer(t, j)
        return remote(o_ref.at[lanes(u, 32), :], out_ref.at[:, here], osend.at[j], orecv.at[j], (d, u))

    lax.fori_loop(0, TABLE - 1, lambda j, c: (out_copy(j).start(), c)[1], 0)
    out_ref[:, here] = o_ref[mine, :]
    lax.fori_loop(0, TABLE - 1, lambda j, c: (cot_copy(j).wait(), c)[1], 0)

    own_cot.wait()
    pos = lax.broadcasted_iota(I32, (D, S), 1)
    g32 = jnp.where(pos < ln, c_ref[...].astype(F32), 0.0)
    g = g32.astype(BF16)
    dm = mm(wo_ref[...], g, NN).astype(BF16).astype(F32)
    dz_ref[0:D, :] = ((dm * nh2 * gmid).astype(BF16).astype(F32) * zd_ref[0:D, :]).astype(BF16)
    dn = dm * u * gmid
    da = r2 * (dn - jnp.mean(dn, axis=0, keepdims=True) - nh2 * jnp.mean(dn * nh2, axis=0, keepdims=True))
    a_ref[...] = da
    for h in range(HEADS):
        vT = p_ref[D + h * hd:D + (h + 1) * hd, :]
        qT = p_ref[2 * D + h * hd:2 * D + (h + 1) * hd, :]
        kT = p_ref[3 * D + h * hd:3 * D + (h + 1) * hd, :]
        dah = a_ref[h * hd:(h + 1) * hd, :].astype(BF16)
        wt = wt_ref[h]
        dw = mm(vT, dah, TN).astype(BF16).astype(F32)
        ds = (dw * sd_ref[h]).astype(BF16)
        for b, val in ((1, mm(dah, wt, NT)), (2, mm(kT, ds, NN)), (3, mm(qT, ds, NT))):
            rows = slice(b * D + h * hd, b * D + (h + 1) * hd)
            dz_ref[rows, :] = (val.astype(BF16).astype(F32) * zd_ref[rows, :]).astype(BF16)
    dnr = mm(w_ref[...], dz_ref[...], NN).astype(BF16).astype(F32) * gin
    x = x_ref[...].astype(F32)
    nh1 = (x - mu) * r1
    de = r1 * (dnr - jnp.mean(dnr, axis=0, keepdims=True) - nh1 * jnp.mean(dnr * nh1, axis=0, keepdims=True))
    g_ref[...] = (de + g32).astype(BF16)


    def grad_copy(j):
        u = table_peer(t, j)
        return remote(g_ref.at[lanes(u, 32), :], home.at[:, lanes(TABLE - 1 - j, 256)], gsend.at[j], grecv.at[j], (d, u))

    lax.fori_loop(1, TABLE, lambda k, c: (grad_copy(TABLE - 1 - k).start(), c)[1], 0)
    home[:, 0:256] = g_ref[mine, :]
    for half in range(2):
        for q in range(1, SIDE):
            id_copy(half, q).wait()

    def row_copy(half, q, n):
        at = lanes(n, CHUNK)
        src, dst = (home.at[0:16, at], ga) if half == 0 else (home.at[16:32, at], gb)
        return remote(src, dst.at[q, :, at], asend.at[half, q, n], arecv.at[half, q, n], (peers(q)[half], t))

    per = CHUNK // 256

    def terms(half, qs, at):
        ids = jnp.concatenate([(idb_ref if half else ida_ref)[q, :, at] for q in qs], axis=1)
        dx, dy = ids >> 13, (ids >> 11) & 3
        owner, fits = (dy + SIDE - yq, dx == xq) if half else (dx + SIDE - xq, dy == yq)
        return jnp.where(fits, (owner & 3) * 8 + ((ids >> 8) & 7), -1), low_bits(ids & 255)

    def both(qs, at, xa, xb, start):
        every = range(SIDE)
        va = scatter_block(*terms(0, qs, at), xa, every)
        vb = scatter_block(*terms(1, qs, at), xb, every)
        acca[...] = va if start else acca[...] + va
        accb[...] = vb if start else accb[...] + vb

    chunks = home.shape[1] // CHUNK
    others = range(1, SIDE)

    def own(n, start):
        at = lanes(n, CHUNK)
        lax.fori_loop(jnp.maximum(n * per, 1), n * per + per, lambda k, e: (grad_copy(TABLE - 1 - k).wait(), e)[1], 0)
        for r in others:
            row_copy(0, r, n).start()
            row_copy(1, r, n).start()
        both((0,), at, home[0:16, at], home[16:32, at], start)

    def gathered(buf, at):
        return jnp.concatenate([buf[q, :, at] for q in others], axis=1)

    def arrive(n):
        for r in others:
            row_copy(0, r, n).wait()
            row_copy(1, r, n).wait()

    def rest(n):
        at = lanes(n, CHUNK)
        arrive(n)
        both(others, at, gathered(ga, at), gathered(gb, at), False)

    def sum_copy(half, q):
        send, recv = (sb, rb) if half else (sa, ra)
        return remote(send.at[q * 128 : (q + 1) * 128, :], recv.at[q], rsend.at[half, q], rrecv.at[half, q],
                      (peers(q)[1 - half], t))

    def last(n):
        at = lanes(n, CHUNK)
        arrive(n)
        rows = [gathered(ga, at), gathered(gb, at)]
        found = [terms(half, others, at) for half in range(2)]
        for parts in ((2, 1), (3, 0)):
            for half, (acc, send) in enumerate(((acca, sa), (accb, sb))):
                value = scatter_block(*found[half], rows[half], parts)
                for k, q in enumerate(parts):
                    block = slice(q * 128, (q + 1) * 128)
                    total = acc[block, :] + value[k * 128 : (k + 1) * 128]
                    if q:
                        send[block, :] = total.astype(BF16)
                    else:
                        acc[block, :] = total
            for q in parts:
                for half in range(2 if q else 0):
                    sum_copy(half, q).start()

    def add(n, c):
        own(n, False)
        rest(n - 1)
        return c

    own(0, True)
    lax.fori_loop(1, chunks, add, 0)
    last(chunks - 1)
    lax.fori_loop(0, TABLE - 1, lambda j, c: (out_copy(j).wait(), c)[1], 0)
    for half, acc, recv in ((0, acca, ra), (1, accb, rb)):
        total = acc[0:128, :]
        for q in range(1, SIDE):
            sum_copy(half, q).wait()
            total = total + recv[q].astype(F32)
        for h in range(8):
            sum_ref[half * 16 : half * 16 + 16, h * 256 : (h + 1) * 256] = total[h * 16 : (h + 1) * 16]


def finish_kernel(out_ref, sum_ref, out_end, sum_end, out_buf, sum_buf, sems):
    moves = []
    for k in range(2):
        for a, (src, buf, dst) in enumerate(((out_ref, out_buf, out_end), (sum_ref, sum_buf, sum_end))):
            at = pl.ds(k * (src.shape[0] // 2), src.shape[0] // 2)
            moves.append((pltpu.make_async_copy(src.at[at], buf.at[at], sems.at[0, a, k]),
                          pltpu.make_async_copy(buf.at[at], dst.at[at], sems.at[1, a, k])))
    for into, _ in moves:
        into.start()
    for into, back in moves:
        into.wait()
        back.start()
    for _, back in moves:
        back.wait()


def finish(out, total):
    HB = pl.BlockSpec(memory_space=pltpu.HBM)
    return pl.pallas_call(
        finish_kernel,
        out_shape=tuple(jax.ShapeDtypeStruct(a.shape, a.dtype) for a in (out, total)),
        in_specs=[HB] * 2,
        out_specs=(HB, HB),
        scratch_shapes=[pltpu.VMEM(out.shape, out.dtype), pltpu.VMEM(total.shape, total.dtype),
                        pltpu.SemaphoreType.DMA((2, 2, 2))],
    )(out, total)


def on_device(item_ids, user_len, emb_table, cotangent, w_uvqk, w_out, gain_in, gain_mid):
    f, n = cotangent.shape
    vocab = emb_table.shape[1]
    D, S = TABLE * f, n // TABLE
    sem = pltpu.SemaphoreType.DMA
    HB = pl.BlockSpec(memory_space=pltpu.HBM)
    V = pltpu.VMEM
    return finish(*pl.pallas_call(
        step_kernel,
        out_shape=(jax.ShapeDtypeStruct((f, n), BF16), jax.ShapeDtypeStruct((f, vocab // lax.axis_size("dp")), F32)),
        in_specs=[HB] * 9,
        out_specs=(VM, VM),
        scratch_shapes=[
            pltpu.SMEM((n,), I32), pltpu.SMEM(user_len.shape, I32), V((1, n), I32), V((1, D), F32), V((1, D), F32),
            V((f, vocab), BF16), V((vocab // 4, 4 * f), F32), V((2, S, 4 * f), F32), V((TABLE, f, S), BF16), V((D, S), BF16), V((D, S), BF16),
            V((D, 4 * D), BF16), V((D, D), BF16), V((4 * D, S), BF16), V((4 * D, S), F32), V((4 * D, S), BF16),
            V((HEADS, S, S), BF16), V((HEADS, S, S), F32), V((D, S), F32), V((D, S), BF16), V((D, S), BF16),
            V((1, n), I32), V((SIDE, 1, n), I32), V((SIDE, 1, n), I32), V((f, n), BF16),
            V((SIDE, 16, n), BF16), V((SIDE, 16, n), BF16), V((512, 256), F32), V((512, 256), F32),
            V((512, 256), BF16), V((512, 256), BF16), V((SIDE, 128, 256), BF16), V((SIDE, 128, 256), BF16), sem((3,)),
            sem((vocab // 4 // PIECE, 4)), sem((5,)),
        ]
        + [sem((TABLE,))] * 4 + [sem((2, SIDE))] * 2 + [sem((TABLE,))] * 4
        + [sem((2, SIDE, n // CHUNK))] * 2 + [sem((2, SIDE))] * 2,
        compiler_params=pltpu.CompilerParams(collective_id=0, has_side_effects=True, vmem_limit_bytes=VMEM_LIMIT),
    )(item_ids, user_len, item_ids.reshape(1, n), emb_table, cotangent, w_uvqk, w_out,
      gain_in.reshape(1, D), gain_mid.reshape(1, D)))


def solution(mesh):
    return jax.shard_map(
        on_device,
        mesh=mesh,
        in_specs=(P("dp"), P("dp"), P("table", None), P("table", "dp"), P(), P(), P(), P()),
        out_specs=(P("table", "dp"), P("table", "dp")),
        check_vma=False,
    )
```

```python
import functools

import jax
import jax.numpy as jnp
from jax import lax
from jax.experimental import pallas as pl
from jax.experimental.pallas import tpu as pltpu
from jax.sharding import PartitionSpec as P

F32, BF16, I32 = jnp.float32, jnp.bfloat16, jnp.int32
MESH = pl.DeviceIdType.MESH
VM = pl.BlockSpec(memory_space=pltpu.VMEM)
SM = pl.BlockSpec(memory_space=pltpu.SMEM)
EPS = 1e-5
HEADS = 8
NN = (((1,), (0,)), ((), ()))
TN = (((0,), (0,)), ((), ()))
NT = (((1,), (1,)), ((), ()))
TABLE = 16
SIDE = 4


def mm(a, b, dims):
    return lax.dot_general(a, b, dims, preferred_element_type=F32)


def sigmoid(z):
    return 0.5 * jnp.tanh(0.5 * z) + 0.5


def place():
    d, t = lax.axis_index("dp"), lax.axis_index("table")
    return d, t, d // SIDE, d % SIDE


def away(j):
    return TABLE // 2 + (1 - 2 * (j % 2)) * ((j + 1) // 2)


def table_peer(t, j):
    return (t + TABLE + away(j)) % TABLE


def table_source(t, j):
    return (t + 2 * TABLE - away(j)) % TABLE


def column(row):
    n = row.shape[1]
    tall = jnp.broadcast_to(row, (128, n)).T
    return jnp.concatenate([tall, tall], axis=1)

CHUNK = 1024


def low_bits(lo):
    k = lo.shape[1]
    low = jnp.broadcast_to(lo.astype(F32).astype(BF16), (256, k))
    row = lax.broadcasted_iota(I32, (256, k), 0).astype(F32).astype(BF16)
    return jnp.where(row == low, jnp.ones((256, k), BF16), jnp.zeros((256, k), BF16))


def scatter_block(hi, oht, g, parts):
    k = g.shape[1]
    hib = jnp.broadcast_to(hi.astype(F32).astype(BF16), (16, k))
    zero = jnp.zeros((16, k), BF16)
    lhs = [jnp.where(hib == jnp.array(8 * p + q, BF16), g, zero) for p in parts for q in range(8)]
    return mm(jnp.concatenate(lhs, axis=0), oht, NT)


PIECE = 2048
VMEM_LIMIT = 60 << 20


def lanes(i, size):
    return pl.ds(pl.multiple_of(i * size, size), size)


def turn_table(table_ref, rows_ref, first, blocks):
    w = 256
    n = rows_ref.shape[0]

    def turn(b, c):
        block = jnp.concatenate(
            [table_ref[:, pl.ds(pl.multiple_of(q * n + b * w, w), w)].astype(F32) for q in range(4)], axis=0
        )
        rows_ref[lanes(b, w), :] = block.T
        return c

    lax.fori_loop(first, first + blocks, turn, 0, unroll=4)


def gather_block(u, sid_ref, ids_ref, rows_ref, picked):
    n = rows_ref.shape[0]
    base = u * 256
    for r in range(256):
        picked[r : r + 1, :] = rows_ref[pl.ds(sid_ref[base + r] & (n - 1), 1), :]
    cols = picked[...].T
    q = jnp.broadcast_to(ids_ref[:, lanes(u, 256)] >> (n.bit_length() - 1), (32, 256))
    acc = cols[0:32]
    for i in range(1, 4):
        acc = jnp.where(q == i, cols[32 * i : 32 * i + 32], acc)
    return acc.astype(BF16)


def step_kernel(sidh_ref, lenh_ref, idsh_ref, tableh_ref, cot_ref, wh_ref, woh_ref, ginh_ref, gmidh_ref,
                out_ref, sum_ref,
                sid_ref, len_ref, ids_ref, gin_ref, gmid_ref, table_ref, rows_ref, picked, stage, x_ref, c_ref, w_ref, wo_ref, p_ref, zd_ref, dz_ref, wt_ref, sd_ref, a_ref,
                o_ref, g_ref, idp_ref, ida_ref, idb_ref, home, ga, gb, acca, accb, sa, sb, ra, rb,
                wsem, tsem, ssem, esend, erecv, csend, crecv, isend, irecv, osend, orecv, gsend, grecv, asend, arecv, rsend, rrecv):
    d, t, xq, yq = place()

    def peers(q):
        return xq * SIDE + (yq + q) % SIDE, ((xq + q) % SIDE) * SIDE + yq

    weights = [pltpu.make_async_copy(wh_ref, w_ref, wsem.at[0]), pltpu.make_async_copy(woh_ref, wo_ref, wsem.at[1])]
    def piece(c, q):
        at = pl.ds(pl.multiple_of(q * rows_ref.shape[0] + c * PIECE, PIECE), PIECE)
        return pltpu.make_async_copy(tableh_ref.at[:, at], table_ref.at[:, at], tsem.at[c, q])

    small = [pltpu.make_async_copy(a, b, ssem.at[i]) for i, (a, b) in enumerate(
        ((sidh_ref, sid_ref), (idsh_ref, ids_ref), (lenh_ref, len_ref), (ginh_ref, gin_ref), (gmidh_ref, gmid_ref)))]
    pieces = rows_ref.shape[0] // PIECE
    for c in range(pieces):
        for q in range(4):
            piece(c, q).start()
        if c == 0:
            for a in small:
                a.start()
    own_cot = pltpu.make_async_copy(cot_ref.at[:, lanes(t, 256)], c_ref.at[lanes(t, 32), :], wsem.at[2])
    own_cot.start()
    for c in weights:
        c.start()
    bar = pltpu.get_barrier_semaphore()

    def signal(j, c):
        pl.semaphore_signal(bar, inc=1, device_id=(d, table_peer(t, j)), device_id_type=MESH)
        return c

    lax.fori_loop(0, TABLE - 1, signal, 0)
    for q in range(1, SIDE):
        for peer in peers(q):
            pl.semaphore_signal(bar, inc=1, device_id=(peer, t), device_id_type=MESH)

    mine = lanes(t, 32)

    def remote(src, dst, send, recv, dev):
        return pltpu.make_async_remote_copy(
            src_ref=src, dst_ref=dst, send_sem=send, recv_sem=recv, device_id=dev, device_id_type=MESH)

    def emb_copy(j):
        return remote(stage.at[j], x_ref.at[mine, :], esend.at[j], erecv.at[j], (d, table_peer(t, j)))

    def cot_copy(j):
        u = table_peer(t, j)
        return remote(cot_ref.at[:, lanes(u, 256)], c_ref.at[mine, :], csend.at[j], crecv.at[j], (d, u))

    def id_copy(half, q):
        dst = ida_ref if half == 0 else idb_ref
        return remote(idp_ref, dst.at[q], isend.at[half, q], irecv.at[half, q], (peers(q)[half], t))

    for c in range(pieces):
        for q in range(4):
            piece(c, q).wait()
        turn_table(table_ref, rows_ref, c * (PIECE // 256), PIECE // 256)
    for c in small[:2]:
        c.wait()

    def pick(i, c):
        blocks = [gather_block(table_peer(t, 2 * i + k), sid_ref, ids_ref, rows_ref, picked.at[k]) for k in range(2)]
        for k in range(2):
            stage[2 * i + k] = blocks[k]

        @pl.when(i == 0)
        def _():
            pl.semaphore_wait(bar, TABLE - 1 + 2 * (SIDE - 1))

        emb_copy(2 * i).start()

        @pl.when(i < TABLE // 2 - 1)
        def _():
            emb_copy(2 * i + 1).start()

        return c

    lax.fori_loop(0, TABLE // 2, pick, 0)
    lax.fori_loop(0, TABLE - 1, lambda j, c: (cot_copy(j).start(), c)[1], 0)

    def order(j, c):
        idp_ref[:, lanes(TABLE - 1 - j, 256)] = ids_ref[:, lanes(table_source(t, j), 256)]
        return c

    lax.fori_loop(0, TABLE, order, 0)
    x_ref[mine, :] = stage[TABLE - 1]
    ida_ref[0] = idp_ref[...]
    idb_ref[0] = idp_ref[...]
    for half in range(2):
        for q in range(1, SIDE):
            id_copy(half, q).start()
    for c in weights + small[2:]:
        c.wait()
    D, S = x_ref.shape
    hd = D // HEADS
    ln = len_ref[lax.axis_index("table")]
    gin = column(gin_ref[...])
    gmid = column(gmid_ref[...])
    key_i = lax.broadcasted_iota(jnp.int32, (S, S), 0)
    qry_i = lax.broadcasted_iota(jnp.int32, (S, S), 1)
    inv = 1.0 / jnp.full((S, S), ln, jnp.int32).astype(F32)
    scale = jnp.where((key_i <= qry_i) & (key_i < ln), inv, 0.0)
    lax.fori_loop(0, TABLE - 1, lambda j, c: (emb_copy(j).wait(), c)[1], 0)

    x = x_ref[...].astype(F32)
    mu = jnp.mean(x, axis=0, keepdims=True)
    cen = x - mu
    r1 = lax.rsqrt(jnp.mean(cen * cen, axis=0, keepdims=True) + EPS)
    normed = (cen * r1 * gin).astype(BF16)
    for b in range(4):
        z = mm(w_ref[:, b * D:(b + 1) * D], normed, TN)
        sg = sigmoid(z)
        p_ref[b * D:(b + 1) * D, :] = (z * sg).astype(BF16)
        zd_ref[b * D:(b + 1) * D, :] = sg * (1.0 + z * (1.0 - sg))
    for h in range(HEADS):
        vT = p_ref[D + h * hd:D + (h + 1) * hd, :]
        qT = p_ref[2 * D + h * hd:2 * D + (h + 1) * hd, :]
        kT = p_ref[3 * D + h * hd:3 * D + (h + 1) * hd, :]
        s = mm(kT, qT, TN) * (hd ** -0.5)
        sg = sigmoid(s)
        wt = (s * sg * scale).astype(BF16)
        wt_ref[h] = wt
        sd_ref[h] = sg * (1.0 + s * (1.0 - sg)) * (scale * hd ** -0.5)
        a_ref[h * hd:(h + 1) * hd, :] = mm(vT, wt, NN)
    a = a_ref[...]
    cen2 = a - jnp.mean(a, axis=0, keepdims=True)
    r2 = lax.rsqrt(jnp.mean(cen2 * cen2, axis=0, keepdims=True) + EPS)
    nh2 = cen2 * r2
    u = p_ref[0:D, :].astype(F32)
    mixed = (nh2 * gmid * u).astype(BF16)
    o_ref[...] = (x_ref[...].astype(F32) + mm(wo_ref[...], mixed, TN)).astype(BF16)
    here = lanes(t, 256)

    def out_copy(j):
        u = table_peer(t, j)
        return remote(o_ref.at[lanes(u, 32), :], out_ref.at[:, here], osend.at[j], orecv.at[j], (d, u))

    lax.fori_loop(0, TABLE - 1, lambda j, c: (out_copy(j).start(), c)[1], 0)
    own_out = pltpu.make_async_copy(o_ref.at[mine, :], out_ref.at[:, here], wsem.at[3])
    own_out.start()
    lax.fori_loop(0, TABLE - 1, lambda j, c: (cot_copy(j).wait(), c)[1], 0)

    own_cot.wait()
    pos = lax.broadcasted_iota(I32, (D, S), 1)
    g32 = jnp.where(pos < ln, c_ref[...].astype(F32), 0.0)
    g = g32.astype(BF16)
    dm = mm(wo_ref[...], g, NN).astype(BF16).astype(F32)
    dz_ref[0:D, :] = ((dm * nh2 * gmid).astype(BF16).astype(F32) * zd_ref[0:D, :]).astype(BF16)
    dn = dm * u * gmid
    da = r2 * (dn - jnp.mean(dn, axis=0, keepdims=True) - nh2 * jnp.mean(dn * nh2, axis=0, keepdims=True))
    a_ref[...] = da
    for h in range(HEADS):
        vT = p_ref[D + h * hd:D + (h + 1) * hd, :]
        qT = p_ref[2 * D + h * hd:2 * D + (h + 1) * hd, :]
        kT = p_ref[3 * D + h * hd:3 * D + (h + 1) * hd, :]
        dah = a_ref[h * hd:(h + 1) * hd, :].astype(BF16)
        wt = wt_ref[h]
        dw = mm(vT, dah, TN).astype(BF16).astype(F32)
        ds = (dw * sd_ref[h]).astype(BF16)
        for b, val in ((1, mm(dah, wt, NT)), (2, mm(kT, ds, NN)), (3, mm(qT, ds, NT))):
            rows = slice(b * D + h * hd, b * D + (h + 1) * hd)
            dz_ref[rows, :] = (val.astype(BF16).astype(F32) * zd_ref[rows, :]).astype(BF16)
    dnr = mm(w_ref[...], dz_ref[...], NN).astype(BF16).astype(F32) * gin
    x = x_ref[...].astype(F32)
    nh1 = (x - mu) * r1
    de = r1 * (dnr - jnp.mean(dnr, axis=0, keepdims=True) - nh1 * jnp.mean(dnr * nh1, axis=0, keepdims=True))
    g_ref[...] = (de + g32).astype(BF16)


    def grad_copy(j):
        u = table_peer(t, j)
        return remote(g_ref.at[lanes(u, 32), :], home.at[:, lanes(TABLE - 1 - j, 256)], gsend.at[j], grecv.at[j], (d, u))

    lax.fori_loop(1, TABLE, lambda k, c: (grad_copy(TABLE - 1 - k).start(), c)[1], 0)
    home[:, 0:256] = g_ref[mine, :]
    for half in range(2):
        for q in range(1, SIDE):
            id_copy(half, q).wait()

    def row_copy(half, q, n):
        at = lanes(n, CHUNK)
        src, dst = (home.at[0:16, at], ga) if half == 0 else (home.at[16:32, at], gb)
        return remote(src, dst.at[q, :, at], asend.at[half, q, n], arecv.at[half, q, n], (peers(q)[half], t))

    per = CHUNK // 256

    def terms(half, qs, at):
        ids = jnp.concatenate([(idb_ref if half else ida_ref)[q, :, at] for q in qs], axis=1)
        dx, dy = ids >> 13, (ids >> 11) & 3
        owner, fits = (dy + SIDE - yq, dx == xq) if half else (dx + SIDE - xq, dy == yq)
        return jnp.where(fits, (owner & 3) * 8 + ((ids >> 8) & 7), -1), low_bits(ids & 255)

    def both(qs, at, xa, xb, start):
        every = range(SIDE)
        va = scatter_block(*terms(0, qs, at), xa, every)
        vb = scatter_block(*terms(1, qs, at), xb, every)
        acca[...] = va if start else acca[...] + va
        accb[...] = vb if start else accb[...] + vb

    chunks = home.shape[1] // CHUNK
    others = (2, 1, 3)

    def own(n, start):
        at = lanes(n, CHUNK)
        lax.fori_loop(jnp.maximum(n * per, 1), n * per + per, lambda k, e: (grad_copy(TABLE - 1 - k).wait(), e)[1], 0)
        for r in others:
            row_copy(0, r, n).start()
            row_copy(1, r, n).start()
        both((0,), at, home[0:16, at], home[16:32, at], start)

    def gathered(buf, at):
        return jnp.concatenate([buf[q, :, at] for q in others], axis=1)

    def arrive(n):
        for r in others:
            row_copy(0, r, n).wait()
            row_copy(1, r, n).wait()

    def rest(n):
        at = lanes(n, CHUNK)
        arrive(n)
        both(others, at, gathered(ga, at), gathered(gb, at), False)

    def sum_copy(half, q):
        send, recv = (sb, rb) if half else (sa, ra)
        return remote(send.at[q * 128 : (q + 1) * 128, :], recv.at[q], rsend.at[half, q], rrecv.at[half, q],
                      (peers(q)[1 - half], t))

    def last(n):
        at = lanes(n, CHUNK)
        arrive(n)
        rows = [gathered(ga, at), gathered(gb, at)]
        found = [terms(half, others, at) for half in range(2)]
        for parts in ((2, 1), (3, 0)):
            for half, (acc, send) in enumerate(((acca, sa), (accb, sb))):
                value = scatter_block(*found[half], rows[half], parts)
                for k, q in enumerate(parts):
                    block = slice(q * 128, (q + 1) * 128)
                    total = acc[block, :] + value[k * 128 : (k + 1) * 128]
                    if q:
                        send[block, :] = total.astype(BF16)
                    else:
                        acc[block, :] = total
            for q in parts:
                for half in range(2 if q else 0):
                    sum_copy(half, q).start()

    def add(n, c):
        own(n, False)
        rest(n - 1)
        return c

    own(0, True)
    lax.fori_loop(1, chunks, add, 0)
    last(chunks - 1)
    lax.fori_loop(0, TABLE - 1, lambda j, c: (out_copy(j).wait(), c)[1], 0)
    own_out.wait()
    for half, acc, recv in ((0, acca, ra), (1, accb, rb)):
        total = acc[0:128, :]
        for q in range(1, SIDE):
            sum_copy(half, q).wait()
            total = total + recv[q].astype(F32)
        for h in range(8):
            sum_ref[half * 16 : half * 16 + 16, h * 256 : (h + 1) * 256] = total[h * 16 : (h + 1) * 16]


def finish_kernel(out_ref, sum_ref, out_end, sum_end, out_buf, sum_buf, sems):
    moves = []
    for k in range(2):
        for a, (src, buf, dst) in enumerate(((out_ref, out_buf, out_end), (sum_ref, sum_buf, sum_end))):
            at = pl.ds(k * (src.shape[0] // 2), src.shape[0] // 2)
            moves.append((pltpu.make_async_copy(src.at[at], buf.at[at], sems.at[0, a, k]),
                          pltpu.make_async_copy(buf.at[at], dst.at[at], sems.at[1, a, k])))
    for into, _ in moves:
        into.start()
    for into, back in moves:
        into.wait()
        back.start()
    for _, back in moves:
        back.wait()


def finish(out, total):
    HB = pl.BlockSpec(memory_space=pltpu.HBM)
    return pl.pallas_call(
        finish_kernel,
        out_shape=tuple(jax.ShapeDtypeStruct(a.shape, a.dtype) for a in (out, total)),
        in_specs=[HB] * 2,
        out_specs=(HB, HB),
        scratch_shapes=[pltpu.VMEM(out.shape, out.dtype), pltpu.VMEM(total.shape, total.dtype),
                        pltpu.SemaphoreType.DMA((2, 2, 2))],
    )(out, total)


def on_device(item_ids, user_len, emb_table, cotangent, w_uvqk, w_out, gain_in, gain_mid):
    f, n = cotangent.shape
    vocab = emb_table.shape[1]
    D, S = TABLE * f, n // TABLE
    sem = pltpu.SemaphoreType.DMA
    HB = pl.BlockSpec(memory_space=pltpu.HBM)
    V = pltpu.VMEM
    return finish(*pl.pallas_call(
        step_kernel,
        out_shape=(jax.ShapeDtypeStruct((f, n), BF16), jax.ShapeDtypeStruct((f, vocab // lax.axis_size("dp")), F32)),
        in_specs=[HB] * 9,
        out_specs=(HB, VM),
        scratch_shapes=[
            pltpu.SMEM((n,), I32), pltpu.SMEM(user_len.shape, I32), V((1, n), I32), V((1, D), F32), V((1, D), F32),
            V((f, vocab), BF16), V((vocab // 4, 4 * f), F32), V((2, S, 4 * f), F32), V((TABLE, f, S), BF16), V((D, S), BF16), V((D, S), BF16),
            V((D, 4 * D), BF16), V((D, D), BF16), V((4 * D, S), BF16), V((4 * D, S), F32), V((4 * D, S), BF16),
            V((HEADS, S, S), BF16), V((HEADS, S, S), F32), V((D, S), F32), V((D, S), BF16), V((D, S), BF16),
            V((1, n), I32), V((SIDE, 1, n), I32), V((SIDE, 1, n), I32), V((f, n), BF16),
            V((SIDE, 16, n), BF16), V((SIDE, 16, n), BF16), V((512, 256), F32), V((512, 256), F32),
            V((512, 256), BF16), V((512, 256), BF16), V((SIDE, 128, 256), BF16), V((SIDE, 128, 256), BF16), sem((4,)),
            sem((vocab // 4 // PIECE, 4)), sem((5,)),
        ]
        + [sem((TABLE,))] * 4 + [sem((2, SIDE))] * 2 + [sem((TABLE,))] * 4
        + [sem((2, SIDE, n // CHUNK))] * 2 + [sem((2, SIDE))] * 2,
        compiler_params=pltpu.CompilerParams(collective_id=0, has_side_effects=True, vmem_limit_bytes=VMEM_LIMIT),
    )(item_ids, user_len, item_ids.reshape(1, n), emb_table, cotangent, w_uvqk, w_out,
      gain_in.reshape(1, D), gain_mid.reshape(1, D)))


def solution(mesh):
    return jax.shard_map(
        on_device,
        mesh=mesh,
        in_specs=(P("dp"), P("dp"), P("table", None), P("table", "dp"), P(), P(), P(), P()),
        out_specs=(P("table", "dp"), P("table", "dp")),
        check_vma=False,
    )
```
